256 devices in a mesh: dp: 64 (over z, y, core), mp: 4 (over x).
Axes of the slice: x: 4, y: 4, z: 8, core: 2. Of those that a mesh axis runs over, the one named last changes fastest.
Arguments:
- attention: bfloat16 [8192, 2048], P('dp', 'mp'), may hold values from -6 to 6
- residual: bfloat16 [8192, 2048], P('dp', 'mp'), may hold values from -6 to 6
- out_weight: bfloat16 [2048, 2048], P('mp', 'dp'), may hold values from -0.125 to 0.125
- ffn_gain: float32 [2048], P('mp'), may hold values from 0.1 to 1.9
- shared_gate: bfloat16 [2048, 2816], P('dp', 'mp'), may hold values from -0.125 to 0.125
- shared_up: bfloat16 [2048, 2816], P('dp', 'mp'), may hold values from -0.125 to 0.125
- shared_down: bfloat16 [2816, 2048], P('mp', 'dp'), may hold values from -0.109375 to 0.109375
- expert_gate: bfloat16 [64, 2048, 1408], P('dp', None, 'mp'), may hold values from -0.125 to 0.125
- expert_up: bfloat16 [64, 2048, 1408], P('dp', None, 'mp'), may hold values from -0.125 to 0.125
- expert_down: bfloat16 [64, 1408, 2048], P('dp', 'mp'), may hold values from -0.15625 to 0.15625
- route_ids: int32 [8192, 6], P('dp'), may hold values from 0 to 63, all different within a row; in each aligned block of 128 rows (0 to 127, 128 to 255, ...) at most 16 rows name the same one
- route_scores: float32 [8192, 6], P('dp'), may hold values from 0.05 to 1
- placement: int32 [64], replicated, may hold values from 0 to 63, each once
- next_gain: float32 [2048], P('mp'), may hold values from 0.1 to 1.9
Outputs:
- final: bfloat16 [8192, 2048], P('dp', 'mp')
- next_normed: bfloat16 [8192, 2048], P('dp', 'mp')
The draws below stay inside these ranges and needn't reach their ends.
Inputs may be any that keep to these rules, and one draw needn't show every extreme that they name: `route_ids`: A token's 6 experts differ. In each aligned block of 128 rows (the rows of one index of dp) no expert is named by more than 16 rows, a bound that some block reaches. `placement`: each storage index is used by exactly one expert.
All inputs are finite; a program needn't handle non-finite values.
Results may differ from the reference program's by a relative error of at most 0.0075.
Values may be sent and summed in bfloat16 or wider, within the bound.
A program may use at most 128 MiB of HBM per device.

```python
import math
import jax
import jax.numpy as jnp
import numpy as np
from jax import lax

D = 2048
FFE = 1408
TOP = 6
TOK_DEV = 128
EXPERTS = 64
SH = 2816
CAP = 16
TOKENS = 8192
N_DP = 64


def level_of(rng, shape, split, least, largest):
    level = 1.0
    for axis_at, shards_of in split:
        heights = jax.random.uniform(jax.random.fold_in(jax.random.fold_in(rng, 6), axis_at), (shards_of,), jnp.float32, least / len(split), largest / len(split))
        level = level * jnp.repeat(jnp.exp(heights), shape[axis_at] // shards_of).reshape((-1,) + (1,) * (len(shape) - 1 - axis_at))
    return level


def assign_block(rng, own, number, rows, number_of, top, limit, slope):
    order = jax.random.permutation(rng, number_of)
    heavy_load, usual = shares(number_of, rows * top, limit, slope, True), shares(number_of, rows * top, limit, slope, False)
    places = jnp.arange(number_of)

    def named(tallies, offset_by):
        used = int((tallies > 0).sum())
        fixed = max(1, used // 4)
        moved = fixed + (places - fixed + offset_by * (used - fixed)) % max(1, number_of - fixed)
        return jnp.zeros((number_of,), jnp.int32).at[order[jnp.where(places < fixed, places, moved)]].set(jnp.asarray(tallies, jnp.int32))

    tallies = jnp.where(number % 4 == 0, named(heavy_load, number // 4), named(usual, number - number // 4 - 1))
    mixed = jax.random.permutation(jax.random.fold_in(own, 3), number_of)
    giver, taker = mixed[0:number_of // 2 * 2:2], mixed[1:number_of // 2 * 2:2]
    margin = jnp.minimum(tallies[giver] - 1, limit - tallies[taker]) // 2
    margin = jnp.where((giver == order[0]) | (taker == order[0]) | (tallies[taker] == 0), 0, jnp.maximum(margin, 0))
    moved = jax.random.randint(jax.random.fold_in(own, 4), (number_of // 2,), 0, 1 << 20) % (margin + 1)
    tallies = tallies.at[giver].add(-moved).at[taker].add(moved)
    labels = jnp.searchsorted(jnp.cumsum(tallies), jnp.arange(rows * top), side="right").astype(jnp.int32)
    grid = labels.reshape(top, rows).T
    grid = grid[jax.random.permutation(jax.random.fold_in(own, 1), rows)]
    offset_by = jax.random.randint(jax.random.fold_in(own, 2), (rows, 1), 0, top)
    return jnp.take_along_axis(grid, (jnp.arange(top)[None, :] + offset_by) % top, axis=1)


def shares(number_of, total, most, skew, full):
    loads = [(1 << 20) // math.isqrt(rank ** skew) + 1 for rank in range(1, number_of + 1)]
    largest = most if full else min(most, max(-(-total // number_of), total * loads[0] // sum(loads)))
    least = 1 if total - largest >= number_of - 1 else 0
    counts, spare = [largest] + [least] * (number_of - 1), total - largest - least * (number_of - 1)
    while spare > 0:
        candidates = [i for i in range(1, number_of) if counts[i] < largest] or [i for i in range(1, number_of) if counts[i] < most]
        whole, remaining = sum([loads[i] for i in candidates]), spare
        for i in candidates:
            more = min(most - counts[i], max(1, remaining * loads[i] // whole), spare)
            counts[i] = counts[i] + more
            spare = spare - more
    return np.array(counts)


def normal_values(rng, shape, deviation, reach, shards=(), kind=jnp.bfloat16):
    array = jax.random.normal(rng, shape, jnp.float32) * deviation
    if len(shards) > 0:
        array = level_of(rng, shape, shards, -0.22, 0.18) * array
    return jnp.clip(array, min=-reach, max=reach).astype(kind)


def setup_inputs(seed: int = 0) -> dict:
    arg_keys = jax.random.split(jax.random.key(seed), 15)
    attention = normal_values(arg_keys[0], (TOKENS, D), 1.0, 6.0, ((0, 64), (1, 4)))
    residual = normal_values(arg_keys[1], (TOKENS, D), 1.0, 6.0, ((0, 64), (1, 4)))
    out_weight = normal_values(arg_keys[2], (D, D), D ** -0.5, 0.125, ((0, 4), (1, 64)))
    ffn_gain = jnp.clip(1.0 + 0.18 * jax.random.normal(arg_keys[3], (D,), jnp.float32), 0.1, 1.9)
    shared_gate = normal_values(arg_keys[4], (D, SH), D ** -0.5, 0.125, ((0, 64), (1, 4)))
    shared_up = normal_values(arg_keys[5], (D, SH), D ** -0.5, 0.125, ((0, 64), (1, 4)))
    shared_down = normal_values(arg_keys[6], (SH, D), SH ** -0.5, 0.109375, ((0, 4), (1, 64)))
    expert_gate = normal_values(arg_keys[7], (EXPERTS, D, FFE), D ** -0.5, 0.125, ((0, 64), (2, 4)))
    expert_up = normal_values(arg_keys[8], (EXPERTS, D, FFE), D ** -0.5, 0.125, ((0, 64), (2, 4)))
    expert_down = normal_values(arg_keys[9], (EXPERTS, FFE, D), FFE ** -0.5, 0.15625, ((0, 64), (1, 4)))
    route_ids_keys = jax.random.split(jax.random.fold_in(arg_keys[10], 1), TOKENS // TOK_DEV)
    route_ids_turns = jax.random.permutation(jax.random.fold_in(arg_keys[10], 3), TOKENS // TOK_DEV)
    route_ids = jax.vmap(lambda own, number: assign_block(jax.random.fold_in(arg_keys[10], 2), own, number, TOK_DEV, EXPERTS, TOP, CAP, 2))(route_ids_keys, route_ids_turns).reshape((TOKENS, TOP))
    route_scores = jnp.clip(jnp.exp(math.log(1.0) - 2.9957323 * jax.random.uniform(arg_keys[11], (TOKENS, TOP), jnp.float32) ** level_of(arg_keys[11], (TOKENS, TOP), ((0, 64),), -0.2, 0.2)), 0.05, 1.0)
    placement = jax.random.permutation(arg_keys[12], EXPERTS).astype(jnp.int32)
    next_gain = jnp.clip(1.0 + 0.18 * jax.random.normal(arg_keys[13], (D,), jnp.float32), 0.1, 1.9)
    return dict(attention=attention, residual=residual, out_weight=out_weight, ffn_gain=ffn_gain, shared_gate=shared_gate, shared_up=shared_up, shared_down=shared_down, expert_gate=expert_gate, expert_up=expert_up, expert_down=expert_down, route_ids=route_ids, route_scores=route_scores, placement=placement, next_gain=next_gain)


def rms_norm(values, gain):
    values = values.astype(jnp.float32)
    mean_sq = lax.optimization_barrier(jnp.mean(values * values, axis=1, keepdims=True))
    return (values * lax.rsqrt(mean_sq + 1e-06) * gain).astype(jnp.bfloat16)

def reference(attention, residual, out_weight, ffn_gain, shared_gate, shared_up, shared_down, expert_gate, expert_up, expert_down, route_ids, route_scores, placement, next_gain):
    projected = jnp.dot(attention, out_weight, preferred_element_type=jnp.float32)
    hidden = (residual.astype(jnp.float32) + projected).astype(jnp.bfloat16)
    normed = rms_norm(hidden, ffn_gain)
    shared_act = (jax.nn.silu(jnp.dot(normed, shared_gate, preferred_element_type=jnp.float32)) * jnp.dot(normed, shared_up, preferred_element_type=jnp.float32)).astype(jnp.bfloat16)
    shared_out = jnp.dot(shared_act, shared_down, preferred_element_type=jnp.float32)
    flat_ids = route_ids.reshape(N_DP, TOK_DEV * TOP)
    one_hot = (flat_ids[:, :, None] == jnp.arange(EXPERTS, dtype=jnp.int32)[None, None, :]).astype(jnp.int32)
    target = lax.optimization_barrier(jnp.sum(one_hot * placement[None, None, :], axis=2))
    slot = lax.optimization_barrier(jnp.sum((jnp.cumsum(one_hot, axis=1) - one_hot) * one_hot, axis=2))
    source = jnp.arange(N_DP, dtype=jnp.int32)[:, None]
    index = ((target * N_DP + source) * CAP + slot).reshape(-1)
    token = (source * TOK_DEV + jnp.arange(TOK_DEV * TOP, dtype=jnp.int32)[None, :] // TOP).reshape(-1)
    token_table = jnp.zeros((EXPERTS * N_DP * CAP,), jnp.int32).at[index].set(token.astype(jnp.int32))
    score_table = jnp.zeros((EXPERTS * N_DP * CAP,), route_scores.dtype).at[index].set(route_scores.reshape(-1))
    token_table = token_table.reshape(EXPERTS, N_DP * CAP)
    score_table = score_table.reshape(EXPERTS, N_DP * CAP)

    def one_expert(total, inputs):
        tokens_here, scores_here, gate_block, up_block, down_block = inputs
        in_rows = normed[tokens_here]
        activated = (jax.nn.silu(jnp.dot(in_rows, gate_block, preferred_element_type=jnp.float32)) * jnp.dot(in_rows, up_block, preferred_element_type=jnp.float32)).astype(jnp.bfloat16)
        out_rows = jnp.dot(activated, down_block, preferred_element_type=jnp.float32).astype(jnp.bfloat16)
        total = total.at[tokens_here].add(out_rows.astype(total.dtype) * scores_here[:, None])
        return (total, None)
    routed, _ = lax.scan(one_expert, jnp.zeros((N_DP * TOK_DEV, D), jnp.float32), (token_table, score_table, expert_gate, expert_up, expert_down))
    final = (hidden.astype(jnp.float32) + (shared_out + routed)).astype(jnp.bfloat16)
    return (final, rms_norm(final, next_gain))
```

```python
import jax
import jax.numpy as jnp
from jax import lax
from jax.sharding import PartitionSpec as P

D = 2048


EPSILON = 1e-06


def matmul(left, right):
    return jnp.dot(left, right, preferred_element_type=jnp.float32)


def local(
    attention,
    residual,
    out_weight,
    ffn_gain,
    shared_gate,
    shared_up,
    shared_down,
    expert_gate,
    expert_up,
    expert_down,
    route_ids,
    route_scores,
    placement,
    next_gain,
):
    tok_rows = attention.shape[0]
    top_count = route_ids.shape[1]
    experts = lax.axis_size("dp")
    capacity = min(tok_rows, 8 * tok_rows // experts)
    model_width = D
    partial_value = matmul(attention, lax.all_gather(out_weight, "dp", axis=1, tiled=True))
    projected = lax.psum_scatter(partial_value, "mp", scatter_dimension=1, tiled=True)
    hidden = (residual.astype(jnp.float32) + projected).astype(jnp.bfloat16)
    hidden_float = hidden.astype(jnp.float32)
    squares = lax.psum(jnp.sum(hidden_float * hidden_float, axis=1), "mp")
    normed = (hidden_float * lax.rsqrt(squares / model_width + EPSILON)[:, None] * ffn_gain).astype(
        jnp.bfloat16
    )
    whole_rows = lax.all_gather(normed, "mp", axis=1, tiled=True)

    flat_ids = route_ids.reshape(-1)
    expert_iota = jnp.arange(experts, dtype=jnp.int32)
    one_hot = (flat_ids[:, None] == expert_iota[None, :]).astype(jnp.int32)
    target = jnp.sum(one_hot * placement[None, :], axis=1)
    slot = jnp.sum((jnp.cumsum(one_hot, axis=0) - one_hot) * one_hot, axis=1)
    dest = target * capacity + slot
    slots = experts * capacity
    hit = (dest[:, None] == jnp.arange(slots, dtype=jnp.int32)[None, :]).reshape(
        tok_rows, top_count, slots
    )
    flat_scores = route_scores.reshape(tok_rows, top_count)
    combine = jnp.sum(jnp.where(hit, flat_scores[:, :, None], 0.0), axis=1)
    pick = jnp.any(hit, axis=1).astype(jnp.bfloat16)
    outgoing = matmul(pick.T, whole_rows).astype(jnp.bfloat16)
    arrived = lax.all_to_all(
        outgoing.reshape(experts, capacity, model_width),
        "dp",
        split_axis=0,
        concat_axis=0,
        tiled=True,
    )
    in_rows = arrived.reshape(slots, model_width)
    gate_val = matmul(in_rows, expert_gate[0])
    up_val = matmul(in_rows, expert_up[0])
    activated = (jax.nn.silu(gate_val) * up_val).astype(jnp.bfloat16)
    partial_out = matmul(activated, expert_down[0]).astype(jnp.bfloat16)
    returned = lax.all_to_all(
        partial_out.reshape(experts, capacity, model_width),
        "dp",
        split_axis=0,
        concat_axis=0,
        tiled=True,
    ).reshape(slots, model_width)
    routed = jnp.dot(
        combine,
        returned.astype(jnp.float32),
        precision=lax.Precision.HIGHEST,
        preferred_element_type=jnp.float32,
    )

    pieces = (
        lax.all_gather(shared_gate, "dp", axis=0, tiled=True),
        lax.all_gather(shared_up, "dp", axis=0, tiled=True),
    )
    shared_gval = matmul(whole_rows, pieces[0])
    shared_uval = matmul(whole_rows, pieces[1])
    shared_act = (jax.nn.silu(shared_gval) * shared_uval).astype(jnp.bfloat16)
    shared_part = matmul(shared_act, lax.all_gather(shared_down, "dp", axis=1, tiled=True))
    mixture = lax.psum_scatter(routed + shared_part, "mp", scatter_dimension=1, tiled=True)
    final = (hidden_float + mixture).astype(jnp.bfloat16)
    final_float = final.astype(jnp.float32)
    final_squares = lax.psum(jnp.sum(final_float * final_float, axis=1), "mp")
    next_normed = (
        final_float * lax.rsqrt(final_squares / model_width + EPSILON)[:, None] * next_gain
    ).astype(jnp.bfloat16)
    return (final, next_normed)


def solution(mesh):
    in_specs = (
        P("dp", "mp"),
        P("dp", "mp"),
        P("mp", "dp"),
        P("mp"),
        P("dp", "mp"),
        P("dp", "mp"),
        P("mp", "dp"),
        P("dp", None, "mp"),
        P("dp", None, "mp"),
        P("dp", "mp", None),
        P("dp", None),
        P("dp", None),
        P(),
        P("mp"),
    )
    out_specs = (P("dp", "mp"), P("dp", "mp"))
    return jax.shard_map(local, mesh=mesh, in_specs=in_specs, out_specs=out_specs, check_vma=False)
```

```python
import jax
import jax.numpy as jnp
from jax import lax
from jax.sharding import PartitionSpec as P

D = 2048


EPSILON = 1e-06


def matmul(left, right):
    return jnp.dot(left, right, preferred_element_type=jnp.float32)


def matmul_t(left, right_t):
    return lax.dot_general(
        left, right_t, (((1,), (1,)), ((), ())), preferred_element_type=jnp.float32
    )


def local(
    attention,
    residual,
    out_weight,
    ffn_gain,
    shared_gate,
    shared_up,
    shared_down,
    expert_gate,
    expert_up,
    expert_down,
    route_ids,
    route_scores,
    placement,
    next_gain,
):
    tok_rows = attention.shape[0]
    top_count = route_ids.shape[1]
    mp_count = lax.axis_size("mp")
    experts = lax.axis_size("dp")
    capacity = min(tok_rows, 8 * tok_rows // experts)
    quarter = capacity // mp_count
    model_width = D
    block_width = model_width // mp_count
    out_weight_t = lax.all_gather(out_weight.T, "dp", axis=0, tiled=True)
    partial_value = matmul_t(attention, out_weight_t)
    projected = lax.psum_scatter(partial_value, "mp", scatter_dimension=1, tiled=True)
    hidden = (residual.astype(jnp.float32) + projected).astype(jnp.bfloat16)
    hidden_float = hidden.astype(jnp.float32)
    whole_hidden = lax.all_gather(hidden, "mp", axis=1, tiled=True).astype(jnp.float32)
    squares = jnp.sum(whole_hidden * whole_hidden, axis=1)
    gain = lax.all_gather(ffn_gain, "mp", axis=0, tiled=True)
    whole_rows = (
        whole_hidden * lax.rsqrt(squares / model_width + EPSILON)[:, None] * gain
    ).astype(jnp.bfloat16)

    flat_ids = route_ids.reshape(-1)
    expert_iota = jnp.arange(experts, dtype=jnp.int32)
    one_hot = (flat_ids[:, None] == expert_iota[None, :]).astype(jnp.int32)
    target = jnp.sum(one_hot * placement[None, :], axis=1)
    slot = jnp.sum((jnp.cumsum(one_hot, axis=0) - one_hot) * one_hot, axis=1)
    dest = target * capacity + slot
    slots = experts * capacity
    hit = (dest[:, None] == jnp.arange(slots, dtype=jnp.int32)[None, :]).reshape(
        tok_rows, top_count, slots
    )
    flat_scores = route_scores.reshape(tok_rows, top_count)
    combine = jnp.sum(jnp.where(hit, flat_scores[:, :, None], 0.0), axis=1)
    pick = jnp.any(hit, axis=1).astype(jnp.bfloat16)
    mine = pick.reshape(tok_rows, experts, mp_count, quarter)[:, :, lax.axis_index("mp"), :]
    outgoing = matmul(mine.reshape(tok_rows, experts * quarter).T, whole_rows).astype(jnp.bfloat16)
    arrived = lax.all_to_all(
        outgoing.reshape(experts, quarter, model_width),
        "dp",
        split_axis=0,
        concat_axis=0,
        tiled=True,
    )
    copies = jnp.broadcast_to(arrived[None], (mp_count, experts, quarter, model_width))
    in_rows = lax.all_to_all(copies, "mp", split_axis=0, concat_axis=0, tiled=True)
    in_rows = in_rows.reshape(mp_count * experts * quarter, model_width)
    gate_val = matmul(in_rows, expert_gate[0])
    up_val = matmul(in_rows, expert_up[0])
    activated = (jax.nn.silu(gate_val) * up_val).astype(jnp.bfloat16)
    partial_out = matmul(activated, expert_down[0]).astype(jnp.bfloat16)
    by_block = partial_out.reshape(mp_count, experts, quarter, mp_count, block_width)
    by_block = jnp.transpose(by_block, (3, 1, 0, 2, 4))
    summed = lax.all_to_all(by_block, "mp", split_axis=0, concat_axis=0, tiled=True)
    expert_out = jnp.sum(summed.astype(jnp.float32), axis=0).astype(jnp.bfloat16)
    returned = lax.all_to_all(
        expert_out, "dp", split_axis=0, concat_axis=0, tiled=True
    ).reshape(slots, block_width)
    routed = jnp.dot(
        combine,
        returned.astype(jnp.float32),
        precision=lax.Precision.HIGHEST,
        preferred_element_type=jnp.float32,
    )

    pieces = (
        lax.all_gather(shared_gate, "dp", axis=0, tiled=True),
        lax.all_gather(shared_up, "dp", axis=0, tiled=True),
    )
    shared_gval = matmul(whole_rows, pieces[0])
    shared_uval = matmul(whole_rows, pieces[1])
    shared_act = (jax.nn.silu(shared_gval) * shared_uval).astype(jnp.bfloat16)
    shared_down_t = lax.all_gather(shared_down.T, "dp", axis=0, tiled=True)
    shared_part = matmul_t(shared_act, shared_down_t)
    mixture = lax.psum_scatter(shared_part, "mp", scatter_dimension=1, tiled=True) + routed
    final = (hidden_float + mixture).astype(jnp.bfloat16)
    final_float = final.astype(jnp.float32)
    final_squares = lax.psum(jnp.sum(final_float * final_float, axis=1), "mp")
    next_normed = (
        final_float * lax.rsqrt(final_squares / model_width + EPSILON)[:, None] * next_gain
    ).astype(jnp.bfloat16)
    return (final, next_normed)


def solution(mesh):
    in_specs = (
        P("dp", "mp"),
        P("dp", "mp"),
        P("mp", "dp"),
        P("mp"),
        P("dp", "mp"),
        P("dp", "mp"),
        P("mp", "dp"),
        P("dp", None, "mp"),
        P("dp", None, "mp"),
        P("dp", "mp", None),
        P("dp", None),
        P("dp", None),
        P(),
        P("mp"),
    )
    out_specs = (P("dp", "mp"), P("dp", "mp"))
    return jax.shard_map(local, mesh=mesh, in_specs=in_specs, out_specs=out_specs, check_vma=False)
```

```python
import functools

import jax
import jax.numpy as jnp
from jax import lax
from jax.experimental import pallas as pl
from jax.experimental.pallas import tpu as pltpu
from jax.sharding import PartitionSpec as P

MESH = pl.DeviceIdType.MESH

D = 2048


EPSILON = 1e-06


def matmul(left, right):
    return jnp.dot(left, right, preferred_element_type=jnp.float32)


def matmul_t(left, right_t):
    return lax.dot_general(
        left, right_t, (((1,), (1,)), ((), ())), preferred_element_type=jnp.float32
    )


def _gather_kernel(n, x_ref, o_ref, send_sem, recv_sem):
    me = lax.axis_index("dp")
    col = lax.axis_index("mp")
    rows = x_ref.shape[0]
    barrier = pltpu.get_barrier_semaphore()

    def greet(p, carry):
        peer = lax.rem(me + p, n)
        pl.semaphore_signal(barrier, inc=1, device_id=(peer, col), device_id_type=MESH)
        return carry

    lax.fori_loop(1, n, greet, 0)
    pl.semaphore_wait(barrier, n - 1)
    own = o_ref.at[pl.ds(me * rows, rows)]
    pltpu.make_async_copy(x_ref, own, recv_sem).start()

    def send(p, carry):
        peer = lax.rem(me + p, n)
        pltpu.make_async_remote_copy(
            src_ref=x_ref,
            dst_ref=own,
            send_sem=send_sem,
            recv_sem=recv_sem,
            device_id=(peer, col),
            device_id_type=MESH,
        ).start()
        return carry

    lax.fori_loop(1, n, send, 0)
    sent = o_ref.at[pl.ds(0, (n - 1) * rows)]
    pltpu.make_async_copy(sent, sent, send_sem).wait()
    pltpu.make_async_copy(o_ref, o_ref, recv_sem).wait()


def gather_dp(x, collective_id):
    n = lax.axis_size("dp")
    rows, cols = x.shape
    return pl.pallas_call(
        functools.partial(_gather_kernel, n),
        out_shape=jax.ShapeDtypeStruct((n * rows, cols), x.dtype),
        in_specs=[pl.BlockSpec(memory_space=pl.ANY)],
        out_specs=pl.BlockSpec(memory_space=pl.ANY),
        scratch_shapes=[pltpu.SemaphoreType.DMA(()), pltpu.SemaphoreType.DMA(())],
        compiler_params=pltpu.CompilerParams(collective_id=collective_id, has_side_effects=True),
    )(x)


def reduce_scatter_mp(value):
    mp_count = lax.axis_size("mp")
    rows, width = value.shape
    blocks = jnp.transpose(value.reshape(rows, mp_count, width // mp_count), (1, 0, 2))
    return jnp.sum(lax.all_to_all(blocks, "mp", split_axis=0, concat_axis=0, tiled=True), axis=0)


def local(
    attention,
    residual,
    out_weight,
    ffn_gain,
    shared_gate,
    shared_up,
    shared_down,
    expert_gate,
    expert_up,
    expert_down,
    route_ids,
    route_scores,
    placement,
    next_gain,
):
    tok_rows = attention.shape[0]
    top_count = route_ids.shape[1]
    mp_count = lax.axis_size("mp")
    experts = lax.axis_size("dp")
    capacity = min(tok_rows, 8 * tok_rows // experts)
    quarter = capacity // mp_count
    model_width = D
    block_width = model_width // mp_count
    out_weight_t = gather_dp(out_weight.T, 0)
    partial_value = matmul_t(attention, out_weight_t)
    projected = reduce_scatter_mp(partial_value)
    hidden = (residual.astype(jnp.float32) + projected).astype(jnp.bfloat16)
    hidden_float = hidden.astype(jnp.float32)
    whole_hidden = lax.all_gather(hidden, "mp", axis=1, tiled=True).astype(jnp.float32)
    squares = jnp.sum(whole_hidden * whole_hidden, axis=1)
    gain = lax.all_gather(ffn_gain, "mp", axis=0, tiled=True)
    whole_rows = (
        whole_hidden * lax.rsqrt(squares / model_width + EPSILON)[:, None] * gain
    ).astype(jnp.bfloat16)

    flat_ids = route_ids.reshape(-1)
    expert_iota = jnp.arange(experts, dtype=jnp.int32)
    one_hot = (flat_ids[:, None] == expert_iota[None, :]).astype(jnp.int32)
    target = jnp.sum(one_hot * placement[None, :], axis=1)
    slot = jnp.sum((jnp.cumsum(one_hot, axis=0) - one_hot) * one_hot, axis=1)
    dest = target * capacity + slot
    slots = experts * capacity
    hit = (dest[:, None] == jnp.arange(slots, dtype=jnp.int32)[None, :]).reshape(
        tok_rows, top_count, slots
    )
    flat_scores = route_scores.reshape(tok_rows, top_count)
    combine = jnp.sum(jnp.where(hit, flat_scores[:, :, None], 0.0), axis=1)
    pick = jnp.any(hit, axis=1).astype(jnp.bfloat16)
    mine = pick.reshape(tok_rows, experts, mp_count, quarter)[:, :, lax.axis_index("mp"), :]
    outgoing = matmul(mine.reshape(tok_rows, experts * quarter).T, whole_rows).astype(jnp.bfloat16)
    arrived = lax.all_to_all(
        outgoing.reshape(experts, quarter, model_width),
        "dp",
        split_axis=0,
        concat_axis=0,
        tiled=True,
    )
    copies = jnp.broadcast_to(arrived[None], (mp_count, experts, quarter, model_width))
    in_rows = lax.all_to_all(copies, "mp", split_axis=0, concat_axis=0, tiled=True)
    in_rows = in_rows.reshape(mp_count * experts * quarter, model_width)
    gate_val = matmul(in_rows, expert_gate[0])
    up_val = matmul(in_rows, expert_up[0])
    activated = (jax.nn.silu(gate_val) * up_val).astype(jnp.bfloat16)
    partial_out = matmul(activated, expert_down[0]).astype(jnp.bfloat16)
    by_block = partial_out.reshape(mp_count, experts, quarter, mp_count, block_width)
    by_block = jnp.transpose(by_block, (3, 1, 0, 2, 4))
    summed = lax.all_to_all(by_block, "mp", split_axis=0, concat_axis=0, tiled=True)
    expert_out = jnp.sum(summed.astype(jnp.float32), axis=0).astype(jnp.bfloat16)
    returned = lax.all_to_all(
        expert_out, "dp", split_axis=0, concat_axis=0, tiled=True
    ).reshape(slots, block_width)
    routed = jnp.dot(
        combine,
        returned.astype(jnp.float32),
        precision=lax.Precision.HIGHEST,
        preferred_element_type=jnp.float32,
    )

    pieces = (
        lax.all_gather(shared_gate, "dp", axis=0, tiled=True),
        lax.all_gather(shared_up, "dp", axis=0, tiled=True),
    )
    shared_gval = matmul(whole_rows, pieces[0])
    shared_uval = matmul(whole_rows, pieces[1])
    shared_act = (jax.nn.silu(shared_gval) * shared_uval).astype(jnp.bfloat16)
    shared_down_t = lax.all_gather(shared_down.T, "dp", axis=0, tiled=True)
    shared_part = matmul_t(shared_act, shared_down_t)
    mixture = reduce_scatter_mp(shared_part) + routed
    final = (hidden_float + mixture).astype(jnp.bfloat16)
    final_float = final.astype(jnp.float32)
    final_squares = lax.psum(jnp.sum(final_float * final_float, axis=1), "mp")
    next_normed = (
        final_float * lax.rsqrt(final_squares / model_width + EPSILON)[:, None] * next_gain
    ).astype(jnp.bfloat16)
    return (final, next_normed)


def solution(mesh):
    in_specs = (
        P("dp", "mp"),
        P("dp", "mp"),
        P("mp", "dp"),
        P("mp"),
        P("dp", "mp"),
        P("dp", "mp"),
        P("mp", "dp"),
        P("dp", None, "mp"),
        P("dp", None, "mp"),
        P("dp", "mp", None),
        P("dp", None),
        P("dp", None),
        P(),
        P("mp"),
    )
    out_specs = (P("dp", "mp"), P("dp", "mp"))
    return jax.shard_map(local, mesh=mesh, in_specs=in_specs, out_specs=out_specs, check_vma=False)
```

```python
import functools

import jax
import jax.numpy as jnp
from jax import lax
from jax.experimental import pallas as pl
from jax.experimental.pallas import tpu as pltpu
from jax.sharding import PartitionSpec as P

MESH = pl.DeviceIdType.MESH

D = 2048


EPSILON = 1e-06


def matmul(left, right):
    return jnp.dot(left, right, preferred_element_type=jnp.float32)


def matmul_t(left, right_t):
    return lax.dot_general(
        left, right_t, (((1,), (1,)), ((), ())), preferred_element_type=jnp.float32
    )


def _gather_kernel(n, x_ref, o_ref, send_sem, recv_sem):
    me = lax.axis_index("dp")
    col = lax.axis_index("mp")
    rows = x_ref.shape[0]
    barrier = pltpu.get_barrier_semaphore()

    def greet(p, carry):
        peer = lax.rem(me + p, n)
        pl.semaphore_signal(barrier, inc=1, device_id=(peer, col), device_id_type=MESH)
        return carry

    lax.fori_loop(1, n, greet, 0)
    pl.semaphore_wait(barrier, n - 1)
    own = o_ref.at[pl.ds(me * rows, rows)]
    pltpu.make_async_copy(x_ref, own, recv_sem).start()

    def send(p, carry):
        peer = lax.rem(me + p, n)
        pltpu.make_async_remote_copy(
            src_ref=x_ref,
            dst_ref=own,
            send_sem=send_sem,
            recv_sem=recv_sem,
            device_id=(peer, col),
            device_id_type=MESH,
        ).start()
        return carry

    lax.fori_loop(1, n, send, 0)
    sent = o_ref.at[pl.ds(0, (n - 1) * rows)]
    pltpu.make_async_copy(sent, sent, send_sem).wait()
    pltpu.make_async_copy(o_ref, o_ref, recv_sem).wait()


def gather_dp(x, collective_id):
    n = lax.axis_size("dp")
    rows, cols = x.shape
    return pl.pallas_call(
        functools.partial(_gather_kernel, n),
        out_shape=jax.ShapeDtypeStruct((n * rows, cols), x.dtype),
        in_specs=[pl.BlockSpec(memory_space=pl.ANY)],
        out_specs=pl.BlockSpec(memory_space=pl.ANY),
        scratch_shapes=[pltpu.SemaphoreType.DMA(()), pltpu.SemaphoreType.DMA(())],
        compiler_params=pltpu.CompilerParams(collective_id=collective_id, has_side_effects=True),
    )(x)


def reduce_scatter_mp(blocks):
    return jnp.sum(lax.all_to_all(blocks, "mp", split_axis=0, concat_axis=0, tiled=True), axis=0)


def local(
    attention,
    residual,
    out_weight,
    ffn_gain,
    shared_gate,
    shared_up,
    shared_down,
    expert_gate,
    expert_up,
    expert_down,
    route_ids,
    route_scores,
    placement,
    next_gain,
):
    tok_rows = attention.shape[0]
    top_count = route_ids.shape[1]
    mp_count = lax.axis_size("mp")
    experts = lax.axis_size("dp")
    capacity = min(tok_rows, 8 * tok_rows // experts)
    model_width = D
    block_width = model_width // mp_count
    out_weight_t = gather_dp(out_weight.T, 0).reshape(mp_count, block_width, -1)
    partial_value = jnp.einsum(
        "tk,qfk->qtf", attention, out_weight_t, preferred_element_type=jnp.float32
    )
    gain_row = jnp.broadcast_to(ffn_gain[None, None, :], (mp_count, 1, block_width))
    exchanged = lax.all_to_all(
        jnp.concatenate([partial_value, gain_row], axis=1),
        "mp",
        split_axis=0,
        concat_axis=0,
        tiled=True,
    )
    projected = jnp.sum(exchanged[:, :tok_rows, :], axis=0)
    gain = exchanged[:, tok_rows, :].reshape(model_width)
    hidden = (residual.astype(jnp.float32) + projected).astype(jnp.bfloat16)
    hidden_float = hidden.astype(jnp.float32)
    whole_hidden = lax.all_gather(hidden, "mp", axis=1, tiled=True).astype(jnp.float32)
    squares = jnp.sum(whole_hidden * whole_hidden, axis=1)
    scale = lax.rsqrt(squares / model_width + EPSILON)[:, None]
    whole_rows = (whole_hidden * scale * gain).astype(jnp.bfloat16)
    normed = (hidden_float * scale * ffn_gain).astype(jnp.bfloat16)

    flat_ids = route_ids.reshape(-1)
    expert_iota = jnp.arange(experts, dtype=jnp.int32)
    one_hot = (flat_ids[:, None] == expert_iota[None, :]).astype(jnp.int32)
    target = jnp.sum(one_hot * placement[None, :], axis=1)
    slot = jnp.sum((jnp.cumsum(one_hot, axis=0) - one_hot) * one_hot, axis=1)
    dest = target * capacity + slot
    slots = experts * capacity
    hit = (dest[:, None] == jnp.arange(slots, dtype=jnp.int32)[None, :]).reshape(
        tok_rows, top_count, slots
    )
    flat_scores = route_scores.reshape(tok_rows, top_count)
    combine = jnp.sum(jnp.where(hit, flat_scores[:, :, None], 0.0), axis=1)
    pick = jnp.any(hit, axis=1).astype(jnp.bfloat16)
    outgoing = matmul(pick.T, normed).astype(jnp.bfloat16)
    arrived = lax.all_to_all(
        outgoing.reshape(experts, capacity, block_width),
        "dp",
        split_axis=0,
        concat_axis=0,
        tiled=True,
    ).reshape(slots, block_width)
    copies = jnp.broadcast_to(arrived[None], (mp_count, slots, block_width))
    in_rows = lax.all_to_all(copies, "mp", split_axis=0, concat_axis=0, tiled=True)
    gate_block = expert_gate[0].reshape(mp_count, block_width, -1)
    up_block = expert_up[0].reshape(mp_count, block_width, -1)
    gate_val = jnp.einsum("qsf,qfh->sh", in_rows, gate_block, preferred_element_type=jnp.float32)
    up_val = jnp.einsum("qsf,qfh->sh", in_rows, up_block, preferred_element_type=jnp.float32)
    activated = (jax.nn.silu(gate_val) * up_val).astype(jnp.bfloat16)
    down_block = expert_down[0].reshape(-1, mp_count, block_width)
    partial_out = jnp.einsum(
        "sh,hqf->qsf", activated, down_block, preferred_element_type=jnp.float32
    ).astype(jnp.bfloat16)
    summed = lax.all_to_all(partial_out, "mp", split_axis=0, concat_axis=0, tiled=True)
    expert_out = jnp.sum(summed.astype(jnp.float32), axis=0).astype(jnp.bfloat16)
    returned = lax.all_to_all(
        expert_out.reshape(experts, capacity, block_width),
        "dp",
        split_axis=0,
        concat_axis=0,
        tiled=True,
    ).reshape(slots, block_width)
    routed = jnp.dot(
        combine,
        returned.astype(jnp.float32),
        precision=lax.Precision.HIGHEST,
        preferred_element_type=jnp.float32,
    )

    pieces = (
        lax.all_gather(shared_gate, "dp", axis=0, tiled=True),
        lax.all_gather(shared_up, "dp", axis=0, tiled=True),
    )
    shared_gval = matmul(whole_rows, pieces[0])
    shared_uval = matmul(whole_rows, pieces[1])
    shared_act = (jax.nn.silu(shared_gval) * shared_uval).astype(jnp.bfloat16)
    shared_down_t = lax.all_gather(shared_down.T, "dp", axis=0, tiled=True)
    shared_part = jnp.einsum(
        "th,qfh->qtf",
        shared_act,
        shared_down_t.reshape(mp_count, block_width, -1),
        preferred_element_type=jnp.float32,
    )
    mixture = reduce_scatter_mp(shared_part) + routed
    final = (hidden_float + mixture).astype(jnp.bfloat16)
    final_float = final.astype(jnp.float32)
    final_squares = lax.psum(jnp.sum(final_float * final_float, axis=1), "mp")
    next_normed = (
        final_float * lax.rsqrt(final_squares / model_width + EPSILON)[:, None] * next_gain
    ).astype(jnp.bfloat16)
    return (final, next_normed)


def solution(mesh):
    in_specs = (
        P("dp", "mp"),
        P("dp", "mp"),
        P("mp", "dp"),
        P("mp"),
        P("dp", "mp"),
        P("dp", "mp"),
        P("mp", "dp"),
        P("dp", None, "mp"),
        P("dp", None, "mp"),
        P("dp", "mp", None),
        P("dp", None),
        P("dp", None),
        P(),
        P("mp"),
    )
    out_specs = (P("dp", "mp"), P("dp", "mp"))
    return jax.shard_map(local, mesh=mesh, in_specs=in_specs, out_specs=out_specs, check_vma=False)
```

```python
import functools

import jax
import jax.numpy as jnp
from jax import lax
from jax.experimental import pallas as pl
from jax.experimental.pallas import tpu as pltpu
from jax.sharding import PartitionSpec as P

MESH = pl.DeviceIdType.MESH

D = 2048


EPSILON = 1e-06


def matmul(left, right):
    return jnp.dot(left, right, preferred_element_type=jnp.float32)


def matmul_t(left, right_t):
    return lax.dot_general(
        left, right_t, (((1,), (1,)), ((), ())), preferred_element_type=jnp.float32
    )


def _gather_kernel(n, x_ref, o_ref, send_sem, recv_sem):
    me = lax.axis_index("dp")
    col = lax.axis_index("mp")
    rows = x_ref.shape[0]
    barrier = pltpu.get_barrier_semaphore()

    def greet(p, carry):
        peer = lax.rem(me + p, n)
        pl.semaphore_signal(barrier, inc=1, device_id=(peer, col), device_id_type=MESH)
        return carry

    lax.fori_loop(1, n, greet, 0)
    pl.semaphore_wait(barrier, n - 1)
    own = o_ref.at[pl.ds(me * rows, rows)]
    pltpu.make_async_copy(x_ref, own, recv_sem).start()

    def send(p, carry):
        peer = lax.rem(me + p, n)
        pltpu.make_async_remote_copy(
            src_ref=x_ref,
            dst_ref=own,
            send_sem=send_sem,
            recv_sem=recv_sem,
            device_id=(peer, col),
            device_id_type=MESH,
        ).start()
        return carry

    lax.fori_loop(1, n, send, 0)
    sent = o_ref.at[pl.ds(0, (n - 1) * rows)]
    pltpu.make_async_copy(sent, sent, send_sem).wait()
    pltpu.make_async_copy(o_ref, o_ref, recv_sem).wait()


def gather_dp(x, collective_id):
    n = lax.axis_size("dp")
    rows, cols = x.shape
    return pl.pallas_call(
        functools.partial(_gather_kernel, n),
        out_shape=jax.ShapeDtypeStruct((n * rows, cols), x.dtype),
        in_specs=[pl.BlockSpec(memory_space=pl.ANY)],
        out_specs=pl.BlockSpec(memory_space=pl.ANY),
        scratch_shapes=[pltpu.SemaphoreType.DMA(()), pltpu.SemaphoreType.DMA(())],
        compiler_params=pltpu.CompilerParams(collective_id=collective_id, has_side_effects=True),
    )(x)


def reduce_scatter_mp(blocks):
    return jnp.sum(lax.all_to_all(blocks, "mp", split_axis=0, concat_axis=0, tiled=True), axis=0)


def local(
    attention,
    residual,
    out_weight,
    ffn_gain,
    shared_gate,
    shared_up,
    shared_down,
    expert_gate,
    expert_up,
    expert_down,
    route_ids,
    route_scores,
    placement,
    next_gain,
):
    tok_rows = attention.shape[0]
    top_count = route_ids.shape[1]
    mp_count = lax.axis_size("mp")
    experts = lax.axis_size("dp")
    capacity = min(tok_rows, 8 * tok_rows // experts)
    model_width = D
    block_width = model_width // mp_count
    out_weight_t = gather_dp(out_weight.T, 0).reshape(mp_count, block_width, -1)
    partial_value = jnp.einsum(
        "tk,qfk->qtf", attention, out_weight_t, preferred_element_type=jnp.float32
    )
    gain_row = jnp.broadcast_to(ffn_gain[None, None, :], (mp_count, 1, block_width))
    exchanged = lax.all_to_all(
        jnp.concatenate([partial_value, gain_row], axis=1),
        "mp",
        split_axis=0,
        concat_axis=0,
        tiled=True,
    )
    projected = jnp.sum(exchanged[:, :tok_rows, :], axis=0)
    gain = exchanged[:, tok_rows, :].reshape(model_width)
    hidden = (residual.astype(jnp.float32) + projected).astype(jnp.bfloat16)
    hidden_float = hidden.astype(jnp.float32)
    whole_hidden = lax.all_gather(hidden, "mp", axis=1, tiled=True).astype(jnp.float32)
    squares = jnp.sum(whole_hidden * whole_hidden, axis=1)
    scale = lax.rsqrt(squares / model_width + EPSILON)[:, None]
    whole_rows = (whole_hidden * scale * gain).astype(jnp.bfloat16)
    normed = (hidden_float * scale * ffn_gain).astype(jnp.bfloat16)

    flat_ids = route_ids.reshape(-1)
    expert_iota = jnp.arange(experts, dtype=jnp.int32)
    one_hot = (flat_ids[:, None] == expert_iota[None, :]).astype(jnp.int32)
    target = jnp.sum(one_hot * placement[None, :], axis=1)
    slot = jnp.sum((jnp.cumsum(one_hot, axis=0) - one_hot) * one_hot, axis=1)
    dest = target * capacity + slot
    slots = experts * capacity
    hit = (dest[:, None] == jnp.arange(slots, dtype=jnp.int32)[None, :]).reshape(
        tok_rows, top_count, slots
    )
    flat_scores = route_scores.reshape(tok_rows, top_count)
    combine = jnp.sum(jnp.where(hit, flat_scores[:, :, None], 0.0), axis=1)
    pick = jnp.any(hit, axis=1).astype(jnp.bfloat16)
    outgoing = matmul(pick.T, normed).astype(jnp.bfloat16)
    arrived = lax.all_to_all(
        outgoing.reshape(experts, capacity, block_width),
        "dp",
        split_axis=0,
        concat_axis=0,
        tiled=True,
    ).reshape(slots, block_width)
    copies = jnp.broadcast_to(arrived[None], (mp_count, slots, block_width))
    in_rows = lax.all_to_all(copies, "mp", split_axis=0, concat_axis=0, tiled=True)
    down_shard, _ = lax.optimization_barrier((shared_down.T, copies))
    shared_down_t = gather_dp(down_shard, 1)
    in_rows, shared_down_t = lax.optimization_barrier((in_rows, shared_down_t))
    gate_block = expert_gate[0].reshape(mp_count, block_width, -1)
    up_block = expert_up[0].reshape(mp_count, block_width, -1)
    gate_val = jnp.einsum("qsf,qfh->sh", in_rows, gate_block, preferred_element_type=jnp.float32)
    up_val = jnp.einsum("qsf,qfh->sh", in_rows, up_block, preferred_element_type=jnp.float32)
    activated = (jax.nn.silu(gate_val) * up_val).astype(jnp.bfloat16)
    down_block = expert_down[0].reshape(-1, mp_count, block_width)
    partial_out = jnp.einsum(
        "sh,hqf->qsf", activated, down_block, preferred_element_type=jnp.float32
    ).astype(jnp.bfloat16)
    summed = lax.all_to_all(partial_out, "mp", split_axis=0, concat_axis=0, tiled=True)
    expert_out = jnp.sum(summed.astype(jnp.float32), axis=0).astype(jnp.bfloat16)
    returned = lax.all_to_all(
        expert_out.reshape(experts, capacity, block_width),
        "dp",
        split_axis=0,
        concat_axis=0,
        tiled=True,
    ).reshape(slots, block_width)
    routed = jnp.dot(
        combine,
        returned.astype(jnp.float32),
        precision=lax.Precision.HIGHEST,
        preferred_element_type=jnp.float32,
    )

    pieces = (
        lax.all_gather(shared_gate, "dp", axis=0, tiled=True),
        lax.all_gather(shared_up, "dp", axis=0, tiled=True),
    )
    shared_gval = matmul(whole_rows, pieces[0])
    shared_uval = matmul(whole_rows, pieces[1])
    shared_act = (jax.nn.silu(shared_gval) * shared_uval).astype(jnp.bfloat16)
    shared_part = jnp.einsum(
        "th,qfh->qtf",
        shared_act,
        shared_down_t.reshape(mp_count, block_width, -1),
        preferred_element_type=jnp.float32,
    )
    mixture = reduce_scatter_mp(shared_part) + routed
    final = (hidden_float + mixture).astype(jnp.bfloat16)
    final_float = final.astype(jnp.float32)
    final_squares = lax.psum(jnp.sum(final_float * final_float, axis=1), "mp")
    next_normed = (
        final_float * lax.rsqrt(final_squares / model_width + EPSILON)[:, None] * next_gain
    ).astype(jnp.bfloat16)
    return (final, next_normed)


def solution(mesh):
    in_specs = (
        P("dp", "mp"),
        P("dp", "mp"),
        P("mp", "dp"),
        P("mp"),
        P("dp", "mp"),
        P("dp", "mp"),
        P("mp", "dp"),
        P("dp", None, "mp"),
        P("dp", None, "mp"),
        P("dp", "mp", None),
        P("dp", None),
        P("dp", None),
        P(),
        P("mp"),
    )
    out_specs = (P("dp", "mp"), P("dp", "mp"))
    return jax.shard_map(local, mesh=mesh, in_specs=in_specs, out_specs=out_specs, check_vma=False)
```

```python
import functools

import jax
import jax.numpy as jnp
from jax import lax
from jax.experimental import pallas as pl
from jax.experimental.pallas import tpu as pltpu
from jax.sharding import Mesh, PartitionSpec as P

MESH = pl.DeviceIdType.MESH

D = 2048


EPSILON = 1e-06


def matmul(left, right):
    return jnp.dot(left, right, preferred_element_type=jnp.float32)


def matmul_t(left, right_t):
    return lax.dot_general(
        left, right_t, (((1,), (1,)), ((), ())), preferred_element_type=jnp.float32
    )


def _gather_kernel(n, x_ref, o_ref, send_sem, recv_sem):
    me = lax.axis_index("g")
    core = lax.axis_index("c")
    col = lax.axis_index("mp")
    rows = x_ref.shape[0]
    barrier = pltpu.get_barrier_semaphore()

    def greet(p, carry):
        peer = lax.rem(me + p, n)
        pl.semaphore_signal(barrier, inc=1, device_id=(peer, core, col), device_id_type=MESH)
        return carry

    lax.fori_loop(1, n, greet, 0)
    pl.semaphore_wait(barrier, n - 1)
    own = o_ref.at[pl.ds(me * rows, rows)]
    pltpu.make_async_copy(x_ref, own, recv_sem).start()

    def send(p, carry):
        peer = lax.rem(me + p, n)
        pltpu.make_async_remote_copy(
            src_ref=x_ref,
            dst_ref=own,
            send_sem=send_sem,
            recv_sem=recv_sem,
            device_id=(peer, core, col),
            device_id_type=MESH,
        ).start()
        return carry

    lax.fori_loop(1, n, send, 0)
    sent = o_ref.at[pl.ds(0, (n - 1) * rows)]
    pltpu.make_async_copy(sent, sent, send_sem).wait()
    pltpu.make_async_copy(o_ref, o_ref, recv_sem).wait()


def gather_g(x, collective_id):
    n = lax.axis_size("g")
    rows, cols = x.shape
    return pl.pallas_call(
        functools.partial(_gather_kernel, n),
        out_shape=jax.ShapeDtypeStruct((n * rows, cols), x.dtype),
        in_specs=[pl.BlockSpec(memory_space=pl.ANY)],
        out_specs=pl.BlockSpec(memory_space=pl.ANY),
        scratch_shapes=[pltpu.SemaphoreType.DMA(()), pltpu.SemaphoreType.DMA(())],
        compiler_params=pltpu.CompilerParams(collective_id=collective_id, has_side_effects=True),
    )(x)


def reduce_scatter_mp(blocks):
    return jnp.sum(lax.all_to_all(blocks, "mp", split_axis=0, concat_axis=0, tiled=True), axis=0)


def swap_halves(value, tok_rows):
    return lax.all_to_all(
        value.reshape(2, tok_rows, value.shape[1]), "c", split_axis=0, concat_axis=0, tiled=True
    )


def natural_blocks(halves, mp_count):
    _, rows, cols = halves.shape
    pairs = lax.axis_size("g")
    width = cols // pairs
    ordered = jnp.transpose(halves.reshape(2, rows, pairs, width), (1, 2, 0, 3))
    return jnp.transpose(ordered.reshape(rows, mp_count, -1), (1, 0, 2))


def local(
    attention,
    residual,
    out_weight,
    ffn_gain,
    shared_gate,
    shared_up,
    shared_down,
    expert_gate,
    expert_up,
    expert_down,
    route_ids,
    route_scores,
    placement,
    next_gain,
):
    dp = ("g", "c")
    tok_rows = attention.shape[0]
    top_count = route_ids.shape[1]
    mp_count = lax.axis_size("mp")
    pairs = lax.axis_size("g")
    experts = pairs * lax.axis_size("c")
    core = lax.axis_index("c")
    capacity = min(tok_rows, 8 * tok_rows // experts)
    model_width = D
    block_width = model_width // mp_count

    w_half = gather_g(out_weight.T, 0)
    att_pair = lax.all_gather(attention, "c", axis=0, tiled=True)
    part_half = matmul_t(att_pair, w_half)
    partial_value = natural_blocks(swap_halves(part_half, tok_rows), mp_count)
    gain_row = jnp.broadcast_to(ffn_gain[None, None, :], (mp_count, 1, block_width))
    exchanged = lax.all_to_all(
        jnp.concatenate([partial_value, gain_row], axis=1),
        "mp",
        split_axis=0,
        concat_axis=0,
        tiled=True,
    )
    projected = jnp.sum(exchanged[:, :tok_rows, :], axis=0)
    gain = exchanged[:, tok_rows, :].reshape(model_width)
    hidden = (residual.astype(jnp.float32) + projected).astype(jnp.bfloat16)
    hidden_float = hidden.astype(jnp.float32)
    whole_hidden = lax.all_gather(hidden, "mp", axis=1, tiled=True).astype(jnp.float32)
    squares = jnp.sum(whole_hidden * whole_hidden, axis=1)
    scale = lax.rsqrt(squares / model_width + EPSILON)[:, None]
    whole_rows = (whole_hidden * scale * gain).astype(jnp.bfloat16)
    normed = (hidden_float * scale * ffn_gain).astype(jnp.bfloat16)

    flat_ids = route_ids.reshape(-1)
    expert_iota = jnp.arange(experts, dtype=jnp.int32)
    one_hot = (flat_ids[:, None] == expert_iota[None, :]).astype(jnp.int32)
    target = jnp.sum(one_hot * placement[None, :], axis=1)
    slot = jnp.sum((jnp.cumsum(one_hot, axis=0) - one_hot) * one_hot, axis=1)
    dest = target * capacity + slot
    slots = experts * capacity
    hit = (dest[:, None] == jnp.arange(slots, dtype=jnp.int32)[None, :]).reshape(
        tok_rows, top_count, slots
    )
    flat_scores = route_scores.reshape(tok_rows, top_count)
    combine = jnp.sum(jnp.where(hit, flat_scores[:, :, None], 0.0), axis=1)
    pick = jnp.any(hit, axis=1).astype(jnp.bfloat16)
    outgoing = matmul(pick.T, normed).astype(jnp.bfloat16)
    arrived = lax.all_to_all(
        outgoing.reshape(experts, capacity, block_width),
        dp,
        split_axis=0,
        concat_axis=0,
        tiled=True,
    ).reshape(slots, block_width)
    copies = jnp.broadcast_to(arrived[None], (mp_count, slots, block_width))
    in_rows = lax.all_to_all(copies, "mp", split_axis=0, concat_axis=0, tiled=True)
    gate_block = expert_gate[0].reshape(mp_count, block_width, -1)
    up_block = expert_up[0].reshape(mp_count, block_width, -1)
    gate_val = jnp.einsum("qsf,qfh->sh", in_rows, gate_block, preferred_element_type=jnp.float32)
    up_val = jnp.einsum("qsf,qfh->sh", in_rows, up_block, preferred_element_type=jnp.float32)
    activated = (jax.nn.silu(gate_val) * up_val).astype(jnp.bfloat16)
    down_block = expert_down[0].reshape(-1, mp_count, block_width)
    partial_out = jnp.einsum(
        "sh,hqf->qsf", activated, down_block, preferred_element_type=jnp.float32
    ).astype(jnp.bfloat16)
    summed = lax.all_to_all(partial_out, "mp", split_axis=0, concat_axis=0, tiled=True)
    expert_out = jnp.sum(summed.astype(jnp.float32), axis=0).astype(jnp.bfloat16)
    returned = lax.all_to_all(
        expert_out.reshape(experts, capacity, block_width),
        dp,
        split_axis=0,
        concat_axis=0,
        tiled=True,
    ).reshape(slots, block_width)
    routed = jnp.dot(
        combine,
        returned.astype(jnp.float32),
        precision=lax.Precision.HIGHEST,
        preferred_element_type=jnp.float32,
    )

    k_block = shared_gate.shape[0]
    hidden_units = shared_gate.shape[1]
    rows_pair = lax.all_gather(whole_rows, "c", axis=0, tiled=True)
    rows_half = lax.dynamic_index_in_dim(
        rows_pair.reshape(2 * tok_rows, pairs, 2, k_block), core, axis=2, keepdims=False
    ).reshape(2 * tok_rows, pairs * k_block)
    gate_half = lax.all_gather(shared_gate, "g", axis=0, tiled=True)
    up_half = lax.all_gather(shared_up, "g", axis=0, tiled=True)
    gate_up = jnp.concatenate([matmul(rows_half, gate_half), matmul(rows_half, up_half)], axis=1)
    gate_up = jnp.sum(swap_halves(gate_up, tok_rows), axis=0)
    shared_act = (
        jax.nn.silu(gate_up[:, :hidden_units]) * gate_up[:, hidden_units:]
    ).astype(jnp.bfloat16)
    act_pair = lax.all_gather(shared_act, "c", axis=0, tiled=True)
    down_half = lax.all_gather(shared_down.T, "g", axis=0, tiled=True)
    shared_part = natural_blocks(swap_halves(matmul_t(act_pair, down_half), tok_rows), mp_count)
    mixture = reduce_scatter_mp(shared_part) + routed
    final = (hidden_float + mixture).astype(jnp.bfloat16)
    final_float = final.astype(jnp.float32)
    final_squares = lax.psum(jnp.sum(final_float * final_float, axis=1), "mp")
    next_normed = (
        final_float * lax.rsqrt(final_squares / model_width + EPSILON)[:, None] * next_gain
    ).astype(jnp.bfloat16)
    return (final, next_normed)


def solution(mesh):
    dp_count, mp_count = mesh.devices.shape
    paired = Mesh(mesh.devices.reshape(dp_count // 2, 2, mp_count), ("g", "c", "mp"))
    dp = ("g", "c")
    in_specs = (
        P(dp, "mp"),
        P(dp, "mp"),
        P("mp", dp),
        P("mp"),
        P(dp, "mp"),
        P(dp, "mp"),
        P("mp", dp),
        P(dp, None, "mp"),
        P(dp, None, "mp"),
        P(dp, "mp", None),
        P(dp, None),
        P(dp, None),
        P(),
        P("mp"),
    )
    out_specs = (P(dp, "mp"), P(dp, "mp"))
    return jax.shard_map(local, mesh=paired, in_specs=in_specs, out_specs=out_specs, check_vma=False)
```

```python
import functools

import jax
import jax.numpy as jnp
from jax import lax
from jax.experimental import pallas as pl
from jax.experimental.pallas import tpu as pltpu
from jax.sharding import Mesh, PartitionSpec as P

MESH = pl.DeviceIdType.MESH

D = 2048


EPSILON = 1e-06


def matmul(left, right):
    return jnp.dot(left, right, preferred_element_type=jnp.float32)


def matmul_t(left, right_t):
    return lax.dot_general(
        left, right_t, (((1,), (1,)), ((), ())), preferred_element_type=jnp.float32
    )


def _gather_kernel(n, x_ref, o_ref, send_sem, recv_sem):
    me = lax.axis_index("g")
    core = lax.axis_index("c")
    col = lax.axis_index("mp")
    rows = x_ref.shape[0]
    barrier = pltpu.get_barrier_semaphore()

    def greet(p, carry):
        peer = lax.rem(me + p, n)
        pl.semaphore_signal(barrier, inc=1, device_id=(peer, core, col), device_id_type=MESH)
        return carry

    lax.fori_loop(1, n, greet, 0)
    pl.semaphore_wait(barrier, n - 1)
    own = o_ref.at[pl.ds(me * rows, rows)]
    pltpu.make_async_copy(x_ref, own, recv_sem).start()

    def send(p, carry):
        peer = lax.rem(me + p, n)
        pltpu.make_async_remote_copy(
            src_ref=x_ref,
            dst_ref=own,
            send_sem=send_sem,
            recv_sem=recv_sem,
            device_id=(peer, core, col),
            device_id_type=MESH,
        ).start()
        return carry

    lax.fori_loop(1, n, send, 0)
    sent = o_ref.at[pl.ds(0, (n - 1) * rows)]
    pltpu.make_async_copy(sent, sent, send_sem).wait()
    pltpu.make_async_copy(o_ref, o_ref, recv_sem).wait()


def gather_g(x, collective_id):
    n = lax.axis_size("g")
    rows, cols = x.shape
    return pl.pallas_call(
        functools.partial(_gather_kernel, n),
        out_shape=jax.ShapeDtypeStruct((n * rows, cols), x.dtype),
        in_specs=[pl.BlockSpec(memory_space=pl.ANY)],
        out_specs=pl.BlockSpec(memory_space=pl.ANY),
        scratch_shapes=[pltpu.SemaphoreType.DMA(()), pltpu.SemaphoreType.DMA(())],
        compiler_params=pltpu.CompilerParams(collective_id=collective_id, has_side_effects=True),
    )(x)


def reduce_scatter_mp(blocks):
    return jnp.sum(lax.all_to_all(blocks, "mp", split_axis=0, concat_axis=0, tiled=True), axis=0)


def swap_halves(value, tok_rows):
    return lax.all_to_all(
        value.reshape(2, tok_rows, value.shape[1]), "c", split_axis=0, concat_axis=0, tiled=True
    )


def natural_blocks(halves, mp_count):
    _, rows, cols = halves.shape
    pairs = lax.axis_size("g")
    width = cols // pairs
    ordered = jnp.transpose(halves.reshape(2, rows, pairs, width), (1, 2, 0, 3))
    return jnp.transpose(ordered.reshape(rows, mp_count, -1), (1, 0, 2))


def local(
    attention,
    residual,
    out_weight,
    ffn_gain,
    shared_gate,
    shared_up,
    shared_down,
    expert_gate,
    expert_up,
    expert_down,
    route_ids,
    route_scores,
    placement,
    next_gain,
):
    dp = ("g", "c")
    tok_rows = attention.shape[0]
    top_count = route_ids.shape[1]
    mp_count = lax.axis_size("mp")
    pairs = lax.axis_size("g")
    experts = pairs * lax.axis_size("c")
    core = lax.axis_index("c")
    capacity = min(tok_rows, 8 * tok_rows // experts)
    model_width = D
    block_width = model_width // mp_count

    w_half = gather_g(out_weight.T, 0)
    att_pair = lax.all_gather(attention, "c", axis=0, tiled=True)
    part_half = matmul_t(att_pair, w_half)
    partial_value = natural_blocks(swap_halves(part_half, tok_rows), mp_count)
    gain_row = jnp.broadcast_to(ffn_gain[None, None, :], (mp_count, 1, block_width))
    exchanged = lax.all_to_all(
        jnp.concatenate([partial_value, gain_row], axis=1),
        "mp",
        split_axis=0,
        concat_axis=0,
        tiled=True,
    )
    projected = jnp.sum(exchanged[:, :tok_rows, :], axis=0)
    gain = exchanged[:, tok_rows, :].reshape(model_width)
    hidden = (residual.astype(jnp.float32) + projected).astype(jnp.bfloat16)
    hidden_float = hidden.astype(jnp.float32)
    whole_hidden = lax.all_gather(hidden, "mp", axis=1, tiled=True).astype(jnp.float32)
    squares = jnp.sum(whole_hidden * whole_hidden, axis=1)
    scale = lax.rsqrt(squares / model_width + EPSILON)[:, None]
    whole_rows = (whole_hidden * scale * gain).astype(jnp.bfloat16)
    normed = (hidden_float * scale * ffn_gain).astype(jnp.bfloat16)

    flat_ids = route_ids.reshape(-1)
    expert_iota = jnp.arange(experts, dtype=jnp.int32)
    one_hot = (flat_ids[:, None] == expert_iota[None, :]).astype(jnp.int32)
    target = jnp.sum(one_hot * placement[None, :], axis=1)
    slot = jnp.sum((jnp.cumsum(one_hot, axis=0) - one_hot) * one_hot, axis=1)
    dest = target * capacity + slot
    slots = experts * capacity
    hit = (dest[:, None] == jnp.arange(slots, dtype=jnp.int32)[None, :]).reshape(
        tok_rows, top_count, slots
    )
    flat_scores = route_scores.reshape(tok_rows, top_count)
    combine = jnp.sum(jnp.where(hit, flat_scores[:, :, None], 0.0), axis=1)
    pick = jnp.any(hit, axis=1).astype(jnp.bfloat16)
    outgoing = matmul(pick.T, normed).astype(jnp.bfloat16)
    arrived = lax.all_to_all(
        outgoing.reshape(experts, capacity, block_width),
        dp,
        split_axis=0,
        concat_axis=0,
        tiled=True,
    ).reshape(slots, block_width)
    copies = jnp.broadcast_to(arrived[None], (mp_count, slots, block_width))
    in_rows = lax.all_to_all(copies, "mp", split_axis=0, concat_axis=0, tiled=True)
    gate_block = expert_gate[0].reshape(mp_count, block_width, -1)
    up_block = expert_up[0].reshape(mp_count, block_width, -1)
    gate_val = jnp.einsum("qsf,qfh->sh", in_rows, gate_block, preferred_element_type=jnp.float32)
    up_val = jnp.einsum("qsf,qfh->sh", in_rows, up_block, preferred_element_type=jnp.float32)
    activated = (jax.nn.silu(gate_val) * up_val).astype(jnp.bfloat16)
    down_block = expert_down[0].reshape(-1, mp_count, block_width)
    partial_out = jnp.einsum(
        "sh,hqf->qsf", activated, down_block, preferred_element_type=jnp.float32
    ).astype(jnp.bfloat16)
    summed = lax.all_to_all(partial_out, "mp", split_axis=0, concat_axis=0, tiled=True)
    expert_out = jnp.sum(summed.astype(jnp.float32), axis=0).astype(jnp.bfloat16)
    returned = lax.all_to_all(
        expert_out.reshape(experts, capacity, block_width),
        dp,
        split_axis=0,
        concat_axis=0,
        tiled=True,
    ).reshape(slots, block_width)
    routed = jnp.dot(
        combine,
        returned.astype(jnp.float32),
        precision=lax.Precision.HIGHEST,
        preferred_element_type=jnp.float32,
    )

    k_block = shared_gate.shape[0]
    hidden_units = shared_gate.shape[1]
    rows_pair = lax.all_gather(whole_rows, "c", axis=0, tiled=True)
    rows_half = lax.dynamic_index_in_dim(
        rows_pair.reshape(2 * tok_rows, pairs, 2, k_block), core, axis=2, keepdims=False
    ).reshape(2 * tok_rows, pairs * k_block)
    shared_half = lax.all_gather(
        jnp.concatenate([shared_gate, shared_up, shared_down.T], axis=1), "g", axis=0, tiled=True
    )
    gate_half = shared_half[:, :hidden_units]
    up_half = shared_half[:, hidden_units : 2 * hidden_units]
    down_half = shared_half[:, 2 * hidden_units :]
    gate_up = jnp.concatenate([matmul(rows_half, gate_half), matmul(rows_half, up_half)], axis=1)
    gate_up = jnp.sum(swap_halves(gate_up, tok_rows), axis=0)
    shared_act = (
        jax.nn.silu(gate_up[:, :hidden_units]) * gate_up[:, hidden_units:]
    ).astype(jnp.bfloat16)
    act_pair = lax.all_gather(shared_act, "c", axis=0, tiled=True)
    shared_part = natural_blocks(swap_halves(matmul_t(act_pair, down_half), tok_rows), mp_count)
    mixture = reduce_scatter_mp(shared_part) + routed
    final = (hidden_float + mixture).astype(jnp.bfloat16)
    final_float = final.astype(jnp.float32)
    final_squares = lax.psum(jnp.sum(final_float * final_float, axis=1), "mp")
    next_normed = (
        final_float * lax.rsqrt(final_squares / model_width + EPSILON)[:, None] * next_gain
    ).astype(jnp.bfloat16)
    return (final, next_normed)


def solution(mesh):
    dp_count, mp_count = mesh.devices.shape
    paired = Mesh(mesh.devices.reshape(dp_count // 2, 2, mp_count), ("g", "c", "mp"))
    dp = ("g", "c")
    in_specs = (
        P(dp, "mp"),
        P(dp, "mp"),
        P("mp", dp),
        P("mp"),
        P(dp, "mp"),
        P(dp, "mp"),
        P("mp", dp),
        P(dp, None, "mp"),
        P(dp, None, "mp"),
        P(dp, "mp", None),
        P(dp, None),
        P(dp, None),
        P(),
        P("mp"),
    )
    out_specs = (P(dp, "mp"), P(dp, "mp"))
    return jax.shard_map(local, mesh=paired, in_specs=in_specs, out_specs=out_specs, check_vma=False)
```

```python
import functools

import jax
import jax.numpy as jnp
from jax import lax
from jax.experimental import pallas as pl
from jax.experimental.pallas import tpu as pltpu
from jax.sharding import Mesh, PartitionSpec as P

MESH = pl.DeviceIdType.MESH

D = 2048


EPSILON = 1e-06


def matmul(left, right):
    return jnp.dot(left, right, preferred_element_type=jnp.float32)


def matmul_t(left, right_t):
    return lax.dot_general(
        left, right_t, (((1,), (1,)), ((), ())), preferred_element_type=jnp.float32
    )


def _gather_kernel(n, x_ref, o_ref, send_sem, recv_sem):
    me = lax.axis_index("g")
    core = lax.axis_index("c")
    col = lax.axis_index("mp")
    rows = x_ref.shape[0]
    barrier = pltpu.get_barrier_semaphore()

    def greet(p, carry):
        peer = lax.rem(me + p, n)
        pl.semaphore_signal(barrier, inc=1, device_id=(peer, core, col), device_id_type=MESH)
        return carry

    lax.fori_loop(1, n, greet, 0)
    pl.semaphore_wait(barrier, n - 1)
    own = o_ref.at[pl.ds(me * rows, rows)]
    pltpu.make_async_copy(x_ref, own, recv_sem).start()

    def send(p, carry):
        peer = lax.rem(me + p, n)
        pltpu.make_async_remote_copy(
            src_ref=x_ref,
            dst_ref=own,
            send_sem=send_sem,
            recv_sem=recv_sem,
            device_id=(peer, core, col),
            device_id_type=MESH,
        ).start()
        return carry

    lax.fori_loop(1, n, send, 0)
    sent = o_ref.at[pl.ds(0, (n - 1) * rows)]
    pltpu.make_async_copy(sent, sent, send_sem).wait()
    pltpu.make_async_copy(o_ref, o_ref, recv_sem).wait()


def gather_g(x, collective_id):
    n = lax.axis_size("g")
    rows, cols = x.shape
    return pl.pallas_call(
        functools.partial(_gather_kernel, n),
        out_shape=jax.ShapeDtypeStruct((n * rows, cols), x.dtype),
        in_specs=[pl.BlockSpec(memory_space=pl.ANY)],
        out_specs=pl.BlockSpec(memory_space=pl.ANY),
        scratch_shapes=[pltpu.SemaphoreType.DMA(()), pltpu.SemaphoreType.DMA(())],
        compiler_params=pltpu.CompilerParams(collective_id=collective_id, has_side_effects=True),
    )(x)


def reduce_scatter_mp(blocks):
    return jnp.sum(lax.all_to_all(blocks, "mp", split_axis=0, concat_axis=0, tiled=True), axis=0)


def swap_halves(value, tok_rows):
    return lax.all_to_all(
        value.reshape(2, tok_rows, value.shape[1]), "c", split_axis=0, concat_axis=0, tiled=True
    )


def natural_blocks(halves, mp_count):
    _, rows, cols = halves.shape
    pairs = lax.axis_size("g")
    width = cols // pairs
    ordered = jnp.transpose(halves.reshape(2, rows, pairs, width), (1, 2, 0, 3))
    return jnp.transpose(ordered.reshape(rows, mp_count, -1), (1, 0, 2))


def local(
    attention,
    residual,
    out_weight,
    ffn_gain,
    shared_gate,
    shared_up,
    shared_down,
    expert_gate,
    expert_up,
    expert_down,
    route_ids,
    route_scores,
    placement,
    next_gain,
):
    dp = ("g", "c")
    tok_rows = attention.shape[0]
    top_count = route_ids.shape[1]
    mp_count = lax.axis_size("mp")
    pairs = lax.axis_size("g")
    experts = pairs * lax.axis_size("c")
    core = lax.axis_index("c")
    capacity = min(tok_rows, 8 * tok_rows // experts)
    model_width = D
    block_width = model_width // mp_count

    w_half = gather_g(out_weight.T, 0)
    att_pair = lax.all_gather(attention, "c", axis=0, tiled=True)
    part_half = matmul_t(att_pair, w_half)
    partial_value = natural_blocks(swap_halves(part_half, tok_rows), mp_count)
    gain_row = jnp.broadcast_to(ffn_gain[None, None, :], (mp_count, 1, block_width))
    exchanged = lax.all_to_all(
        jnp.concatenate([partial_value, gain_row], axis=1),
        "mp",
        split_axis=0,
        concat_axis=0,
        tiled=True,
    )
    projected = jnp.sum(exchanged[:, :tok_rows, :], axis=0)
    gain = exchanged[:, tok_rows, :].reshape(model_width)
    hidden = (residual.astype(jnp.float32) + projected).astype(jnp.bfloat16)
    hidden_float = hidden.astype(jnp.float32)
    whole_hidden = lax.all_gather(hidden, "mp", axis=1, tiled=True).astype(jnp.float32)
    squares = jnp.sum(whole_hidden * whole_hidden, axis=1)
    scale = lax.rsqrt(squares / model_width + EPSILON)[:, None]
    whole_rows = (whole_hidden * scale * gain).astype(jnp.bfloat16)
    normed = (hidden_float * scale * ffn_gain).astype(jnp.bfloat16)

    flat_ids = route_ids.reshape(-1)
    expert_iota = jnp.arange(experts, dtype=jnp.int32)
    one_hot = (flat_ids[:, None] == expert_iota[None, :]).astype(jnp.int32)
    target = jnp.sum(one_hot * placement[None, :], axis=1)
    slot = jnp.sum((jnp.cumsum(one_hot, axis=0) - one_hot) * one_hot, axis=1)
    dest = target * capacity + slot
    slots = experts * capacity
    hit = (dest[:, None] == jnp.arange(slots, dtype=jnp.int32)[None, :]).reshape(
        tok_rows, top_count, slots
    )
    flat_scores = route_scores.reshape(tok_rows, top_count)
    combine = jnp.sum(jnp.where(hit, flat_scores[:, :, None], 0.0), axis=1)
    pick = jnp.any(hit, axis=1).astype(jnp.bfloat16)
    outgoing = matmul(pick.T, normed).astype(jnp.bfloat16)
    arrived = lax.all_to_all(
        outgoing.reshape(experts, capacity, block_width),
        dp,
        split_axis=0,
        concat_axis=0,
        tiled=True,
    ).reshape(slots, block_width)
    copies = jnp.broadcast_to(arrived[None], (mp_count, slots, block_width))
    in_rows = lax.all_to_all(copies, "mp", split_axis=0, concat_axis=0, tiled=True)
    gate_block = expert_gate[0].reshape(mp_count, block_width, -1)
    up_block = expert_up[0].reshape(mp_count, block_width, -1)
    gate_val = jnp.einsum("qsf,qfh->sh", in_rows, gate_block, preferred_element_type=jnp.float32)
    up_val = jnp.einsum("qsf,qfh->sh", in_rows, up_block, preferred_element_type=jnp.float32)
    activated = (jax.nn.silu(gate_val) * up_val).astype(jnp.bfloat16)
    down_block = expert_down[0].reshape(-1, mp_count, block_width)
    partial_out = jnp.einsum(
        "sh,hqf->qsf", activated, down_block, preferred_element_type=jnp.float32
    ).astype(jnp.bfloat16)
    summed = lax.all_to_all(partial_out, "mp", split_axis=0, concat_axis=0, tiled=True)
    expert_out = jnp.sum(summed.astype(jnp.float32), axis=0).astype(jnp.bfloat16)
    returned = lax.all_to_all(
        expert_out.reshape(experts, capacity, block_width),
        dp,
        split_axis=0,
        concat_axis=0,
        tiled=True,
    ).reshape(slots, block_width)
    routed = jnp.dot(
        combine,
        returned.astype(jnp.float32),
        precision=lax.Precision.HIGHEST,
        preferred_element_type=jnp.float32,
    )

    hidden_units = shared_gate.shape[1]
    shared_all = lax.all_gather(
        jnp.concatenate([shared_gate, shared_up, shared_down.T], axis=1), dp, axis=0, tiled=True
    )
    shared_gval = matmul(whole_rows, shared_all[:, :hidden_units])
    shared_uval = matmul(whole_rows, shared_all[:, hidden_units : 2 * hidden_units])
    shared_act = (jax.nn.silu(shared_gval) * shared_uval).astype(jnp.bfloat16)
    shared_part = jnp.einsum(
        "th,qfh->qtf",
        shared_act,
        shared_all[:, 2 * hidden_units :].reshape(mp_count, block_width, hidden_units),
        preferred_element_type=jnp.float32,
    )
    mixture = reduce_scatter_mp(shared_part) + routed
    final = (hidden_float + mixture).astype(jnp.bfloat16)
    final_float = final.astype(jnp.float32)
    final_squares = lax.psum(jnp.sum(final_float * final_float, axis=1), "mp")
    next_normed = (
        final_float * lax.rsqrt(final_squares / model_width + EPSILON)[:, None] * next_gain
    ).astype(jnp.bfloat16)
    return (final, next_normed)


def solution(mesh):
    dp_count, mp_count = mesh.devices.shape
    paired = Mesh(mesh.devices.reshape(dp_count // 2, 2, mp_count), ("g", "c", "mp"))
    dp = ("g", "c")
    in_specs = (
        P(dp, "mp"),
        P(dp, "mp"),
        P("mp", dp),
        P("mp"),
        P(dp, "mp"),
        P(dp, "mp"),
        P("mp", dp),
        P(dp, None, "mp"),
        P(dp, None, "mp"),
        P(dp, "mp", None),
        P(dp, None),
        P(dp, None),
        P(),
        P("mp"),
    )
    out_specs = (P(dp, "mp"), P(dp, "mp"))
    return jax.shard_map(local, mesh=paired, in_specs=in_specs, out_specs=out_specs, check_vma=False)
```

```python
import functools

import jax
import jax.numpy as jnp
from jax import lax
from jax.experimental import pallas as pl
from jax.experimental.pallas import tpu as pltpu
from jax.sharding import Mesh, PartitionSpec as P

MESH = pl.DeviceIdType.MESH

D = 2048


EPSILON = 1e-06


def matmul(left, right):
    return jnp.dot(left, right, preferred_element_type=jnp.float32)


def matmul_t(left, right_t):
    return lax.dot_general(
        left, right_t, (((1,), (1,)), ((), ())), preferred_element_type=jnp.float32
    )


def _gather_kernel(n, x_ref, o_ref, send_sem, recv_sem):
    me = lax.axis_index("g")
    core = lax.axis_index("c")
    col = lax.axis_index("mp")
    rows = x_ref.shape[0]
    barrier = pltpu.get_barrier_semaphore()

    def greet(p, carry):
        peer = lax.rem(me + p, n)
        pl.semaphore_signal(barrier, inc=1, device_id=(peer, core, col), device_id_type=MESH)
        return carry

    lax.fori_loop(1, n, greet, 0)
    pl.semaphore_wait(barrier, n - 1)
    own = o_ref.at[pl.ds(me * rows, rows)]
    pltpu.make_async_copy(x_ref, own, recv_sem).start()

    def send(p, carry):
        peer = lax.rem(me + p, n)
        pltpu.make_async_remote_copy(
            src_ref=x_ref,
            dst_ref=own,
            send_sem=send_sem,
            recv_sem=recv_sem,
            device_id=(peer, core, col),
            device_id_type=MESH,
        ).start()
        return carry

    lax.fori_loop(1, n, send, 0)
    sent = o_ref.at[pl.ds(0, (n - 1) * rows)]
    pltpu.make_async_copy(sent, sent, send_sem).wait()
    pltpu.make_async_copy(o_ref, o_ref, recv_sem).wait()


def gather_g(x, collective_id):
    n = lax.axis_size("g")
    rows, cols = x.shape
    return pl.pallas_call(
        functools.partial(_gather_kernel, n),
        out_shape=jax.ShapeDtypeStruct((n * rows, cols), x.dtype),
        in_specs=[pl.BlockSpec(memory_space=pl.ANY)],
        out_specs=pl.BlockSpec(memory_space=pl.ANY),
        scratch_shapes=[pltpu.SemaphoreType.DMA(()), pltpu.SemaphoreType.DMA(())],
        compiler_params=pltpu.CompilerParams(collective_id=collective_id, has_side_effects=True),
    )(x)


def reduce_scatter_mp(blocks):
    return jnp.sum(lax.all_to_all(blocks, "mp", split_axis=0, concat_axis=0, tiled=True), axis=0)


def swap_halves(value, tok_rows):
    return lax.all_to_all(
        value.reshape(2, tok_rows, value.shape[1]), "c", split_axis=0, concat_axis=0, tiled=True
    )


def natural_blocks(halves, mp_count):
    _, rows, cols = halves.shape
    pairs = lax.axis_size("g")
    width = cols // pairs
    ordered = jnp.transpose(halves.reshape(2, rows, pairs, width), (1, 2, 0, 3))
    return jnp.transpose(ordered.reshape(rows, mp_count, -1), (1, 0, 2))


def local(
    attention,
    residual,
    out_weight,
    ffn_gain,
    shared_gate,
    shared_up,
    shared_down,
    expert_gate,
    expert_up,
    expert_down,
    route_ids,
    route_scores,
    placement,
    next_gain,
):
    dp = ("g", "c")
    tok_rows = attention.shape[0]
    top_count = route_ids.shape[1]
    mp_count = lax.axis_size("mp")
    pairs = lax.axis_size("g")
    experts = pairs * lax.axis_size("c")
    core = lax.axis_index("c")
    capacity = min(tok_rows, 8 * tok_rows // experts)
    model_width = D
    block_width = model_width // mp_count

    w_half = gather_g(out_weight.T, 0)
    att_pair = lax.all_gather(attention, "c", axis=0, tiled=True)
    part_half = matmul_t(att_pair, w_half)
    partial_value = natural_blocks(swap_halves(part_half, tok_rows), mp_count)
    gain_row = jnp.broadcast_to(ffn_gain[None, None, :], (mp_count, 1, block_width))
    exchanged = lax.all_to_all(
        jnp.concatenate([partial_value, gain_row], axis=1),
        "mp",
        split_axis=0,
        concat_axis=0,
        tiled=True,
    )
    projected = jnp.sum(exchanged[:, :tok_rows, :], axis=0)
    gain = exchanged[:, tok_rows, :].reshape(model_width)
    hidden = (residual.astype(jnp.float32) + projected).astype(jnp.bfloat16)
    hidden_float = hidden.astype(jnp.float32)
    whole_hidden = lax.all_gather(hidden, "mp", axis=1, tiled=True).astype(jnp.float32)
    squares = jnp.sum(whole_hidden * whole_hidden, axis=1)
    scale = lax.rsqrt(squares / model_width + EPSILON)[:, None]
    whole_rows = (whole_hidden * scale * gain).astype(jnp.bfloat16)

    flat_ids = route_ids.reshape(-1)
    expert_iota = jnp.arange(experts, dtype=jnp.int32)
    one_hot = (flat_ids[:, None] == expert_iota[None, :]).astype(jnp.int32)
    target = jnp.sum(one_hot * placement[None, :], axis=1)
    slot = jnp.sum((jnp.cumsum(one_hot, axis=0) - one_hot) * one_hot, axis=1)
    dest = target * capacity + slot
    slots = experts * capacity
    hit = (dest[:, None] == jnp.arange(slots, dtype=jnp.int32)[None, :]).reshape(
        tok_rows, top_count, slots
    )
    flat_scores = route_scores.reshape(tok_rows, top_count)
    combine = jnp.sum(jnp.where(hit, flat_scores[:, :, None], 0.0), axis=1)
    pick = jnp.any(hit, axis=1).astype(jnp.bfloat16)
    outgoing = matmul(pick.T, whole_rows).astype(jnp.bfloat16)
    in_rows = lax.all_to_all(
        outgoing.reshape(experts, capacity, model_width),
        dp,
        split_axis=0,
        concat_axis=0,
        tiled=True,
    ).reshape(slots, model_width)
    gate_val = matmul(in_rows, expert_gate[0])
    up_val = matmul(in_rows, expert_up[0])
    activated = (jax.nn.silu(gate_val) * up_val).astype(jnp.bfloat16)
    partial_out = matmul(activated, expert_down[0]).astype(jnp.bfloat16)
    returned = lax.all_to_all(
        partial_out.reshape(experts, capacity, model_width),
        dp,
        split_axis=0,
        concat_axis=0,
        tiled=True,
    ).reshape(slots, model_width)
    routed = jnp.dot(
        combine,
        returned.astype(jnp.float32),
        precision=lax.Precision.HIGHEST,
        preferred_element_type=jnp.float32,
    )

    hidden_units = shared_gate.shape[1]
    shared_all = lax.all_gather(
        jnp.concatenate([shared_gate, shared_up, shared_down.T], axis=1), dp, axis=0, tiled=True
    )
    shared_gval = matmul(whole_rows, shared_all[:, :hidden_units])
    shared_uval = matmul(whole_rows, shared_all[:, hidden_units : 2 * hidden_units])
    shared_act = (jax.nn.silu(shared_gval) * shared_uval).astype(jnp.bfloat16)
    shared_part = jnp.einsum(
        "th,qfh->qtf",
        shared_act,
        shared_all[:, 2 * hidden_units :].reshape(mp_count, block_width, hidden_units),
        preferred_element_type=jnp.float32,
    )
    routed_blocks = jnp.transpose(routed.reshape(tok_rows, mp_count, block_width), (1, 0, 2))
    mixture = reduce_scatter_mp(shared_part + routed_blocks)
    final = (hidden_float + mixture).astype(jnp.bfloat16)
    final_float = final.astype(jnp.float32)
    final_squares = lax.psum(jnp.sum(final_float * final_float, axis=1), "mp")
    next_normed = (
        final_float * lax.rsqrt(final_squares / model_width + EPSILON)[:, None] * next_gain
    ).astype(jnp.bfloat16)
    return (final, next_normed)


def solution(mesh):
    dp_count, mp_count = mesh.devices.shape
    paired = Mesh(mesh.devices.reshape(dp_count // 2, 2, mp_count), ("g", "c", "mp"))
    dp = ("g", "c")
    in_specs = (
        P(dp, "mp"),
        P(dp, "mp"),
        P("mp", dp),
        P("mp"),
        P(dp, "mp"),
        P(dp, "mp"),
        P("mp", dp),
        P(dp, None, "mp"),
        P(dp, None, "mp"),
        P(dp, "mp", None),
        P(dp, None),
        P(dp, None),
        P(),
        P("mp"),
    )
    out_specs = (P(dp, "mp"), P(dp, "mp"))
    return jax.shard_map(local, mesh=paired, in_specs=in_specs, out_specs=out_specs, check_vma=False)
```

```python
import functools

import jax
import jax.numpy as jnp
from jax import lax
from jax.experimental import pallas as pl
from jax.experimental.pallas import tpu as pltpu
from jax.sharding import Mesh, PartitionSpec as P

MESH = pl.DeviceIdType.MESH

D = 2048


EPSILON = 1e-06


def matmul(left, right):
    return jnp.dot(left, right, preferred_element_type=jnp.float32)


def matmul_t(left, right_t):
    return lax.dot_general(
        left, right_t, (((1,), (1,)), ((), ())), preferred_element_type=jnp.float32
    )


def _gather_kernel(axis, x_ref, o_ref, send_sem, recv_sem):
    coords = {name: lax.axis_index(name) for name in ("g", "c", "mp")}
    n = lax.axis_size(axis)
    me = coords[axis]
    rows = x_ref.shape[0]

    def device(peer):
        return tuple(peer if name == axis else coords[name] for name in ("g", "c", "mp"))

    barrier = pltpu.get_barrier_semaphore()

    def greet(p, carry):
        peer = lax.rem(me + p, n)
        pl.semaphore_signal(barrier, inc=1, device_id=device(peer), device_id_type=MESH)
        return carry

    lax.fori_loop(1, n, greet, 0)
    pl.semaphore_wait(barrier, n - 1)
    own = o_ref.at[pl.ds(me * rows, rows)]
    pltpu.make_async_copy(x_ref, own, recv_sem).start()

    def send(p, carry):
        peer = lax.rem(me + p, n)
        pltpu.make_async_remote_copy(
            src_ref=x_ref,
            dst_ref=own,
            send_sem=send_sem,
            recv_sem=recv_sem,
            device_id=device(peer),
            device_id_type=MESH,
        ).start()
        return carry

    lax.fori_loop(1, n, send, 0)
    sent = o_ref.at[pl.ds(0, (n - 1) * rows)]
    pltpu.make_async_copy(sent, sent, send_sem).wait()
    pltpu.make_async_copy(o_ref, o_ref, recv_sem).wait()


def gather_rows(x, axis, collective_id):
    n = lax.axis_size(axis)
    rows, cols = x.shape
    return pl.pallas_call(
        functools.partial(_gather_kernel, axis),
        out_shape=jax.ShapeDtypeStruct((n * rows, cols), x.dtype),
        in_specs=[pl.BlockSpec(memory_space=pl.ANY)],
        out_specs=pl.BlockSpec(memory_space=pl.ANY),
        scratch_shapes=[pltpu.SemaphoreType.DMA(()), pltpu.SemaphoreType.DMA(())],
        compiler_params=pltpu.CompilerParams(collective_id=collective_id, has_side_effects=True),
    )(x)


def reduce_scatter_mp(blocks):
    return jnp.sum(lax.all_to_all(blocks, "mp", split_axis=0, concat_axis=0, tiled=True), axis=0)


def swap_halves(value, tok_rows):
    return lax.all_to_all(
        value.reshape(2, tok_rows, value.shape[1]), "c", split_axis=0, concat_axis=0, tiled=True
    )


def natural_blocks(halves, mp_count):
    _, rows, cols = halves.shape
    pairs = lax.axis_size("g")
    width = cols // pairs
    ordered = jnp.transpose(halves.reshape(2, rows, pairs, width), (1, 2, 0, 3))
    return jnp.transpose(ordered.reshape(rows, mp_count, -1), (1, 0, 2))


def local(
    attention,
    residual,
    out_weight,
    ffn_gain,
    shared_gate,
    shared_up,
    shared_down,
    expert_gate,
    expert_up,
    expert_down,
    route_ids,
    route_scores,
    placement,
    next_gain,
):
    dp = ("g", "c")
    tok_rows = attention.shape[0]
    top_count = route_ids.shape[1]
    mp_count = lax.axis_size("mp")
    pairs = lax.axis_size("g")
    experts = pairs * lax.axis_size("c")
    core = lax.axis_index("c")
    capacity = min(tok_rows, 8 * tok_rows // experts)
    model_width = D
    block_width = model_width // mp_count

    w_half = gather_rows(out_weight.T, "g", 0)
    att_pair = lax.all_gather(attention, "c", axis=0, tiled=True)
    part_half = matmul_t(att_pair, w_half)
    partial_value = natural_blocks(swap_halves(part_half, tok_rows), mp_count)
    gain_row = jnp.broadcast_to(ffn_gain[None, None, :], (mp_count, 1, block_width))
    exchanged = lax.all_to_all(
        jnp.concatenate([partial_value, gain_row], axis=1),
        "mp",
        split_axis=0,
        concat_axis=0,
        tiled=True,
    )
    projected = jnp.sum(exchanged[:, :tok_rows, :], axis=0)
    gain = exchanged[:, tok_rows, :].reshape(model_width)
    hidden = (residual.astype(jnp.float32) + projected).astype(jnp.bfloat16)
    hidden_float = hidden.astype(jnp.float32)
    hidden_blocks = gather_rows(hidden, "mp", 1).reshape(mp_count, tok_rows, block_width)
    whole_hidden = jnp.transpose(hidden_blocks, (1, 0, 2)).reshape(tok_rows, model_width)
    whole_hidden = whole_hidden.astype(jnp.float32)
    squares = jnp.sum(whole_hidden * whole_hidden, axis=1)
    scale = lax.rsqrt(squares / model_width + EPSILON)[:, None]
    whole_rows = (whole_hidden * scale * gain).astype(jnp.bfloat16)
    normed = (hidden_float * scale * ffn_gain).astype(jnp.bfloat16)

    flat_ids = route_ids.reshape(-1)
    expert_iota = jnp.arange(experts, dtype=jnp.int32)
    one_hot = (flat_ids[:, None] == expert_iota[None, :]).astype(jnp.int32)
    target = jnp.sum(one_hot * placement[None, :], axis=1)
    slot = jnp.sum((jnp.cumsum(one_hot, axis=0) - one_hot) * one_hot, axis=1)
    dest = target * capacity + slot
    slots = experts * capacity
    hit = (dest[:, None] == jnp.arange(slots, dtype=jnp.int32)[None, :]).reshape(
        tok_rows, top_count, slots
    )
    flat_scores = route_scores.reshape(tok_rows, top_count)
    combine = jnp.sum(jnp.where(hit, flat_scores[:, :, None], 0.0), axis=1)
    pick = jnp.any(hit, axis=1).astype(jnp.bfloat16)
    outgoing = matmul(pick.T, normed).astype(jnp.bfloat16)
    arrived = lax.all_to_all(
        outgoing.reshape(experts, capacity, block_width),
        dp,
        split_axis=0,
        concat_axis=0,
        tiled=True,
    ).reshape(slots, block_width)
    copies = jnp.broadcast_to(arrived[None], (mp_count, slots, block_width))
    in_rows = lax.all_to_all(copies, "mp", split_axis=0, concat_axis=0, tiled=True)
    gate_block = expert_gate[0].reshape(mp_count, block_width, -1)
    up_block = expert_up[0].reshape(mp_count, block_width, -1)
    gate_val = jnp.einsum("qsf,qfh->sh", in_rows, gate_block, preferred_element_type=jnp.float32)
    up_val = jnp.einsum("qsf,qfh->sh", in_rows, up_block, preferred_element_type=jnp.float32)
    activated = (jax.nn.silu(gate_val) * up_val).astype(jnp.bfloat16)
    down_block = expert_down[0].reshape(-1, mp_count, block_width)
    partial_out = jnp.einsum(
        "sh,hqf->qsf", activated, down_block, preferred_element_type=jnp.float32
    ).astype(jnp.bfloat16)
    summed = lax.all_to_all(partial_out, "mp", split_axis=0, concat_axis=0, tiled=True)
    expert_out = jnp.sum(summed.astype(jnp.float32), axis=0).astype(jnp.bfloat16)
    returned = lax.all_to_all(
        expert_out.reshape(experts, capacity, block_width),
        dp,
        split_axis=0,
        concat_axis=0,
        tiled=True,
    ).reshape(slots, block_width)
    routed = jnp.dot(
        combine,
        returned.astype(jnp.float32),
        precision=lax.Precision.HIGHEST,
        preferred_element_type=jnp.float32,
    )

    hidden_units = shared_gate.shape[1]
    shared_all = lax.all_gather(
        jnp.concatenate([shared_gate, shared_up, shared_down.T], axis=1), dp, axis=0, tiled=True
    )
    shared_gval = matmul(whole_rows, shared_all[:, :hidden_units])
    shared_uval = matmul(whole_rows, shared_all[:, hidden_units : 2 * hidden_units])
    shared_act = (jax.nn.silu(shared_gval) * shared_uval).astype(jnp.bfloat16)
    shared_part = jnp.einsum(
        "th,qfh->qtf",
        shared_act,
        shared_all[:, 2 * hidden_units :].reshape(mp_count, block_width, hidden_units),
        preferred_element_type=jnp.float32,
    )
    mixture = reduce_scatter_mp(shared_part) + routed
    final = (hidden_float + mixture).astype(jnp.bfloat16)
    final_float = final.astype(jnp.float32)
    own_squares = jnp.sum(final_float * final_float, axis=1)
    square_rows = jnp.broadcast_to(own_squares[None, :], (8, tok_rows))
    final_squares = jnp.sum(
        gather_rows(square_rows, "mp", 2).reshape(mp_count, 8, tok_rows)[:, 0, :], axis=0
    )
    next_normed = (
        final_float * lax.rsqrt(final_squares / model_width + EPSILON)[:, None] * next_gain
    ).astype(jnp.bfloat16)
    return (final, next_normed)


def solution(mesh):
    dp_count, mp_count = mesh.devices.shape
    paired = Mesh(mesh.devices.reshape(dp_count // 2, 2, mp_count), ("g", "c", "mp"))
    dp = ("g", "c")
    in_specs = (
        P(dp, "mp"),
        P(dp, "mp"),
        P("mp", dp),
        P("mp"),
        P(dp, "mp"),
        P(dp, "mp"),
        P("mp", dp),
        P(dp, None, "mp"),
        P(dp, None, "mp"),
        P(dp, "mp", None),
        P(dp, None),
        P(dp, None),
        P(),
        P("mp"),
    )
    out_specs = (P(dp, "mp"), P(dp, "mp"))
    return jax.shard_map(local, mesh=paired, in_specs=in_specs, out_specs=out_specs, check_vma=False)
```

```python
import functools

import jax
import jax.numpy as jnp
from jax import lax
from jax.experimental import pallas as pl
from jax.experimental.pallas import tpu as pltpu
from jax.sharding import Mesh, PartitionSpec as P

MESH = pl.DeviceIdType.MESH

D = 2048


EPSILON = 1e-06


def matmul(left, right):
    return jnp.dot(left, right, preferred_element_type=jnp.float32)


def matmul_t(left, right_t):
    return lax.dot_general(
        left, right_t, (((1,), (1,)), ((), ())), preferred_element_type=jnp.float32
    )


def _gather_kernel(axis, x_ref, o_ref, send_sem, recv_sem):
    coords = {name: lax.axis_index(name) for name in ("g", "c", "mp")}
    n = lax.axis_size(axis)
    me = coords[axis]
    rows = x_ref.shape[0]

    def device(peer):
        return tuple(peer if name == axis else coords[name] for name in ("g", "c", "mp"))

    barrier = pltpu.get_barrier_semaphore()

    def greet(p, carry):
        peer = lax.rem(me + p, n)
        pl.semaphore_signal(barrier, inc=1, device_id=device(peer), device_id_type=MESH)
        return carry

    lax.fori_loop(1, n, greet, 0)
    pl.semaphore_wait(barrier, n - 1)
    own = o_ref.at[pl.ds(me * rows, rows)]
    pltpu.make_async_copy(x_ref, own, recv_sem).start()

    def send(p, carry):
        peer = lax.rem(me + p, n)
        pltpu.make_async_remote_copy(
            src_ref=x_ref,
            dst_ref=own,
            send_sem=send_sem,
            recv_sem=recv_sem,
            device_id=device(peer),
            device_id_type=MESH,
        ).start()
        return carry

    lax.fori_loop(1, n, send, 0)
    sent = o_ref.at[pl.ds(0, (n - 1) * rows)]
    pltpu.make_async_copy(sent, sent, send_sem).wait()
    pltpu.make_async_copy(o_ref, o_ref, recv_sem).wait()


def gather_rows(x, axis, collective_id):
    n = lax.axis_size(axis)
    rows, cols = x.shape
    return pl.pallas_call(
        functools.partial(_gather_kernel, axis),
        out_shape=jax.ShapeDtypeStruct((n * rows, cols), x.dtype),
        in_specs=[pl.BlockSpec(memory_space=pl.ANY)],
        out_specs=pl.BlockSpec(memory_space=pl.ANY),
        scratch_shapes=[pltpu.SemaphoreType.DMA(()), pltpu.SemaphoreType.DMA(())],
        compiler_params=pltpu.CompilerParams(collective_id=collective_id, has_side_effects=True),
    )(x)


def _exchange_kernel(axis, x_ref, o_ref, send_sem, recv_sem):
    coords = {name: lax.axis_index(name) for name in ("g", "c", "mp")}
    n = lax.axis_size(axis)
    me = coords[axis]

    def device(peer):
        return tuple(peer if name == axis else coords[name] for name in ("g", "c", "mp"))

    barrier = pltpu.get_barrier_semaphore()

    def greet(p, carry):
        peer = lax.rem(me + p, n)
        pl.semaphore_signal(barrier, inc=1, device_id=device(peer), device_id_type=MESH)
        return carry

    lax.fori_loop(1, n, greet, 0)
    pl.semaphore_wait(barrier, n - 1)
    pltpu.make_async_copy(x_ref.at[me], o_ref.at[me], recv_sem).start()

    def send(p, carry):
        peer = lax.rem(me + p, n)
        pltpu.make_async_remote_copy(
            src_ref=x_ref.at[peer],
            dst_ref=o_ref.at[me],
            send_sem=send_sem,
            recv_sem=recv_sem,
            device_id=device(peer),
            device_id_type=MESH,
        ).start()
        return carry

    lax.fori_loop(1, n, send, 0)
    sent = o_ref.at[pl.ds(0, n - 1)]
    pltpu.make_async_copy(sent, sent, send_sem).wait()
    pltpu.make_async_copy(o_ref, o_ref, recv_sem).wait()


def exchange(x, axis, collective_id):
    return pl.pallas_call(
        functools.partial(_exchange_kernel, axis),
        out_shape=jax.ShapeDtypeStruct(x.shape, x.dtype),
        in_specs=[pl.BlockSpec(memory_space=pl.ANY)],
        out_specs=pl.BlockSpec(memory_space=pl.ANY),
        scratch_shapes=[pltpu.SemaphoreType.DMA(()), pltpu.SemaphoreType.DMA(())],
        compiler_params=pltpu.CompilerParams(collective_id=collective_id, has_side_effects=True),
    )(x)


def reduce_scatter_mp(blocks, collective_id):
    return jnp.sum(exchange(blocks, "mp", collective_id), axis=0)


def swap_halves(value, tok_rows):
    return lax.all_to_all(
        value.reshape(2, tok_rows, value.shape[1]), "c", split_axis=0, concat_axis=0, tiled=True
    )


def natural_blocks(halves, mp_count):
    _, rows, cols = halves.shape
    pairs = lax.axis_size("g")
    width = cols // pairs
    ordered = jnp.transpose(halves.reshape(2, rows, pairs, width), (1, 2, 0, 3))
    return jnp.transpose(ordered.reshape(rows, mp_count, -1), (1, 0, 2))


def local(
    attention,
    residual,
    out_weight,
    ffn_gain,
    shared_gate,
    shared_up,
    shared_down,
    expert_gate,
    expert_up,
    expert_down,
    route_ids,
    route_scores,
    placement,
    next_gain,
):
    dp = ("g", "c")
    tok_rows = attention.shape[0]
    top_count = route_ids.shape[1]
    mp_count = lax.axis_size("mp")
    pairs = lax.axis_size("g")
    experts = pairs * lax.axis_size("c")
    core = lax.axis_index("c")
    capacity = min(tok_rows, 8 * tok_rows // experts)
    model_width = D
    block_width = model_width // mp_count

    w_half = gather_rows(out_weight.T, "g", 0)
    att_pair = lax.all_gather(attention, "c", axis=0, tiled=True)
    part_half = matmul_t(att_pair, w_half)
    partial_value = natural_blocks(swap_halves(part_half, tok_rows), mp_count)
    gain_row = jnp.broadcast_to(ffn_gain[None, None, :], (mp_count, 1, block_width))
    exchanged = exchange(jnp.concatenate([partial_value, gain_row], axis=1), "mp", 3)
    projected = jnp.sum(exchanged[:, :tok_rows, :], axis=0)
    gain = exchanged[:, tok_rows, :].reshape(model_width)
    hidden = (residual.astype(jnp.float32) + projected).astype(jnp.bfloat16)
    hidden_float = hidden.astype(jnp.float32)
    hidden_blocks = gather_rows(hidden, "mp", 1).reshape(mp_count, tok_rows, block_width)
    whole_hidden = jnp.transpose(hidden_blocks, (1, 0, 2)).reshape(tok_rows, model_width)
    whole_hidden = whole_hidden.astype(jnp.float32)
    squares = jnp.sum(whole_hidden * whole_hidden, axis=1)
    scale = lax.rsqrt(squares / model_width + EPSILON)[:, None]
    whole_rows = (whole_hidden * scale * gain).astype(jnp.bfloat16)
    normed = (hidden_float * scale * ffn_gain).astype(jnp.bfloat16)

    flat_ids = route_ids.reshape(-1)
    expert_iota = jnp.arange(experts, dtype=jnp.int32)
    one_hot = (flat_ids[:, None] == expert_iota[None, :]).astype(jnp.int32)
    target = jnp.sum(one_hot * placement[None, :], axis=1)
    slot = jnp.sum((jnp.cumsum(one_hot, axis=0) - one_hot) * one_hot, axis=1)
    dest = target * capacity + slot
    slots = experts * capacity
    hit = (dest[:, None] == jnp.arange(slots, dtype=jnp.int32)[None, :]).reshape(
        tok_rows, top_count, slots
    )
    flat_scores = route_scores.reshape(tok_rows, top_count)
    combine = jnp.sum(jnp.where(hit, flat_scores[:, :, None], 0.0), axis=1)
    pick = jnp.any(hit, axis=1).astype(jnp.bfloat16)
    outgoing = matmul(pick.T, normed).astype(jnp.bfloat16)
    arrived = lax.all_to_all(
        outgoing.reshape(experts, capacity, block_width),
        dp,
        split_axis=0,
        concat_axis=0,
        tiled=True,
    ).reshape(slots, block_width)
    copies = jnp.broadcast_to(arrived[None], (mp_count, slots, block_width))
    in_rows = lax.all_to_all(copies, "mp", split_axis=0, concat_axis=0, tiled=True)
    gate_block = expert_gate[0].reshape(mp_count, block_width, -1)
    up_block = expert_up[0].reshape(mp_count, block_width, -1)
    gate_val = jnp.einsum("qsf,qfh->sh", in_rows, gate_block, preferred_element_type=jnp.float32)
    up_val = jnp.einsum("qsf,qfh->sh", in_rows, up_block, preferred_element_type=jnp.float32)
    activated = (jax.nn.silu(gate_val) * up_val).astype(jnp.bfloat16)
    down_block = expert_down[0].reshape(-1, mp_count, block_width)
    partial_out = jnp.einsum(
        "sh,hqf->qsf", activated, down_block, preferred_element_type=jnp.float32
    ).astype(jnp.bfloat16)
    summed = lax.all_to_all(partial_out, "mp", split_axis=0, concat_axis=0, tiled=True)
    expert_out = jnp.sum(summed.astype(jnp.float32), axis=0).astype(jnp.bfloat16)
    returned = lax.all_to_all(
        expert_out.reshape(experts, capacity, block_width),
        dp,
        split_axis=0,
        concat_axis=0,
        tiled=True,
    ).reshape(slots, block_width)
    routed = jnp.dot(
        combine,
        returned.astype(jnp.float32),
        precision=lax.Precision.HIGHEST,
        preferred_element_type=jnp.float32,
    )

    hidden_units = shared_gate.shape[1]
    shared_all = lax.all_gather(
        jnp.concatenate([shared_gate, shared_up, shared_down.T], axis=1), dp, axis=0, tiled=True
    )
    shared_gval = matmul(whole_rows, shared_all[:, :hidden_units])
    shared_uval = matmul(whole_rows, shared_all[:, hidden_units : 2 * hidden_units])
    shared_act = (jax.nn.silu(shared_gval) * shared_uval).astype(jnp.bfloat16)
    shared_part = jnp.einsum(
        "th,qfh->qtf",
        shared_act,
        shared_all[:, 2 * hidden_units :].reshape(mp_count, block_width, hidden_units),
        preferred_element_type=jnp.float32,
    )
    mixture = reduce_scatter_mp(shared_part, 4) + routed
    final = (hidden_float + mixture).astype(jnp.bfloat16)
    final_float = final.astype(jnp.float32)
    own_squares = jnp.sum(final_float * final_float, axis=1)
    square_rows = jnp.broadcast_to(own_squares[None, :], (8, tok_rows))
    final_squares = jnp.sum(
        gather_rows(square_rows, "mp", 2).reshape(mp_count, 8, tok_rows)[:, 0, :], axis=0
    )
    next_normed = (
        final_float * lax.rsqrt(final_squares / model_width + EPSILON)[:, None] * next_gain
    ).astype(jnp.bfloat16)
    return (final, next_normed)


def solution(mesh):
    dp_count, mp_count = mesh.devices.shape
    paired = Mesh(mesh.devices.reshape(dp_count // 2, 2, mp_count), ("g", "c", "mp"))
    dp = ("g", "c")
    in_specs = (
        P(dp, "mp"),
        P(dp, "mp"),
        P("mp", dp),
        P("mp"),
        P(dp, "mp"),
        P(dp, "mp"),
        P("mp", dp),
        P(dp, None, "mp"),
        P(dp, None, "mp"),
        P(dp, "mp", None),
        P(dp, None),
        P(dp, None),
        P(),
        P("mp"),
    )
    out_specs = (P(dp, "mp"), P(dp, "mp"))
    return jax.shard_map(local, mesh=paired, in_specs=in_specs, out_specs=out_specs, check_vma=False)
```

```python
import functools

import jax
import jax.numpy as jnp
from jax import lax
from jax.experimental import pallas as pl
from jax.experimental.pallas import tpu as pltpu
from jax.sharding import Mesh, PartitionSpec as P

MESH = pl.DeviceIdType.MESH

D = 2048


EPSILON = 1e-06


def matmul(left, right):
    return jnp.dot(left, right, preferred_element_type=jnp.float32)


def matmul_t(left, right_t):
    return lax.dot_general(
        left, right_t, (((1,), (1,)), ((), ())), preferred_element_type=jnp.float32
    )


def _gather_kernel(axis, x_ref, o_ref, send_sem, recv_sem):
    coords = {name: lax.axis_index(name) for name in ("g", "c", "mp")}
    n = lax.axis_size(axis)
    me = coords[axis]
    rows = x_ref.shape[0]

    def device(peer):
        return tuple(peer if name == axis else coords[name] for name in ("g", "c", "mp"))

    barrier = pltpu.get_barrier_semaphore()

    def greet(p, carry):
        peer = lax.rem(me + p, n)
        pl.semaphore_signal(barrier, inc=1, device_id=device(peer), device_id_type=MESH)
        return carry

    lax.fori_loop(1, n, greet, 0)
    pl.semaphore_wait(barrier, n - 1)
    own = o_ref.at[pl.ds(me * rows, rows)]
    pltpu.make_async_copy(x_ref, own, recv_sem).start()

    def send(p, carry):
        peer = lax.rem(me + p, n)
        pltpu.make_async_remote_copy(
            src_ref=x_ref,
            dst_ref=own,
            send_sem=send_sem,
            recv_sem=recv_sem,
            device_id=device(peer),
            device_id_type=MESH,
        ).start()
        return carry

    lax.fori_loop(1, n, send, 0)
    sent = o_ref.at[pl.ds(0, (n - 1) * rows)]
    pltpu.make_async_copy(sent, sent, send_sem).wait()
    pltpu.make_async_copy(o_ref, o_ref, recv_sem).wait()


def gather_rows(x, axis, collective_id):
    n = lax.axis_size(axis)
    rows, cols = x.shape
    return pl.pallas_call(
        functools.partial(_gather_kernel, axis),
        out_shape=jax.ShapeDtypeStruct((n * rows, cols), x.dtype),
        in_specs=[pl.BlockSpec(memory_space=pl.ANY)],
        out_specs=pl.BlockSpec(memory_space=pl.ANY),
        scratch_shapes=[pltpu.SemaphoreType.DMA(()), pltpu.SemaphoreType.DMA(())],
        compiler_params=pltpu.CompilerParams(collective_id=collective_id, has_side_effects=True),
    )(x)


def _exchange_kernel(axis, x_ref, o_ref, send_sem, recv_sem):
    coords = {name: lax.axis_index(name) for name in ("g", "c", "mp")}
    if axis == "dp":
        cores = lax.axis_size("c")
        n = lax.axis_size("g") * cores
        me = coords["g"] * cores + coords["c"]

        def device(peer):
            return (peer // cores, peer % cores, coords["mp"])

    else:
        n = lax.axis_size(axis)
        me = coords[axis]

        def device(peer):
            return tuple(peer if name == axis else coords[name] for name in ("g", "c", "mp"))

    barrier = pltpu.get_barrier_semaphore()

    def greet(p, carry):
        peer = lax.rem(me + p, n)
        pl.semaphore_signal(barrier, inc=1, device_id=device(peer), device_id_type=MESH)
        return carry

    lax.fori_loop(1, n, greet, 0)
    pl.semaphore_wait(barrier, n - 1)
    pltpu.make_async_copy(x_ref.at[me], o_ref.at[me], recv_sem).start()

    def send(p, carry):
        peer = lax.rem(me + p, n)
        pltpu.make_async_remote_copy(
            src_ref=x_ref.at[peer],
            dst_ref=o_ref.at[me],
            send_sem=send_sem,
            recv_sem=recv_sem,
            device_id=device(peer),
            device_id_type=MESH,
        ).start()
        return carry

    lax.fori_loop(1, n, send, 0)
    sent = o_ref.at[pl.ds(0, n - 1)]
    pltpu.make_async_copy(sent, sent, send_sem).wait()
    pltpu.make_async_copy(o_ref, o_ref, recv_sem).wait()


def exchange(x, axis, collective_id):
    return pl.pallas_call(
        functools.partial(_exchange_kernel, axis),
        out_shape=jax.ShapeDtypeStruct(x.shape, x.dtype),
        in_specs=[pl.BlockSpec(memory_space=pl.ANY)],
        out_specs=pl.BlockSpec(memory_space=pl.ANY),
        scratch_shapes=[pltpu.SemaphoreType.DMA(()), pltpu.SemaphoreType.DMA(())],
        compiler_params=pltpu.CompilerParams(collective_id=collective_id, has_side_effects=True),
    )(x)


def reduce_scatter_mp(blocks, collective_id):
    return jnp.sum(exchange(blocks, "mp", collective_id), axis=0)


def swap_halves(value, tok_rows):
    return lax.all_to_all(
        value.reshape(2, tok_rows, value.shape[1]), "c", split_axis=0, concat_axis=0, tiled=True
    )


def natural_blocks(halves, mp_count):
    _, rows, cols = halves.shape
    pairs = lax.axis_size("g")
    width = cols // pairs
    ordered = jnp.transpose(halves.reshape(2, rows, pairs, width), (1, 2, 0, 3))
    return jnp.transpose(ordered.reshape(rows, mp_count, -1), (1, 0, 2))


def local(
    attention,
    residual,
    out_weight,
    ffn_gain,
    shared_gate,
    shared_up,
    shared_down,
    expert_gate,
    expert_up,
    expert_down,
    route_ids,
    route_scores,
    placement,
    next_gain,
):
    dp = ("g", "c")
    tok_rows = attention.shape[0]
    top_count = route_ids.shape[1]
    mp_count = lax.axis_size("mp")
    pairs = lax.axis_size("g")
    experts = pairs * lax.axis_size("c")
    core = lax.axis_index("c")
    capacity = min(tok_rows, 8 * tok_rows // experts)
    model_width = D
    block_width = model_width // mp_count

    w_half = gather_rows(out_weight.T, "g", 0)
    att_pair = lax.all_gather(attention, "c", axis=0, tiled=True)
    part_half = matmul_t(att_pair, w_half)
    partial_value = natural_blocks(swap_halves(part_half, tok_rows), mp_count)
    gain_row = jnp.broadcast_to(ffn_gain[None, None, :], (mp_count, 1, block_width))
    exchanged = exchange(jnp.concatenate([partial_value, gain_row], axis=1), "mp", 3)
    projected = jnp.sum(exchanged[:, :tok_rows, :], axis=0)
    gain = exchanged[:, tok_rows, :].reshape(model_width)
    hidden = (residual.astype(jnp.float32) + projected).astype(jnp.bfloat16)
    hidden_float = hidden.astype(jnp.float32)
    hidden_blocks = gather_rows(hidden, "mp", 1).reshape(mp_count, tok_rows, block_width)
    whole_hidden = jnp.transpose(hidden_blocks, (1, 0, 2)).reshape(tok_rows, model_width)
    whole_hidden = whole_hidden.astype(jnp.float32)
    squares = jnp.sum(whole_hidden * whole_hidden, axis=1)
    scale = lax.rsqrt(squares / model_width + EPSILON)[:, None]
    whole_rows = (whole_hidden * scale * gain).astype(jnp.bfloat16)
    normed = (hidden_float * scale * ffn_gain).astype(jnp.bfloat16)

    flat_ids = route_ids.reshape(-1)
    expert_iota = jnp.arange(experts, dtype=jnp.int32)
    one_hot = (flat_ids[:, None] == expert_iota[None, :]).astype(jnp.int32)
    target = jnp.sum(one_hot * placement[None, :], axis=1)
    slot = jnp.sum((jnp.cumsum(one_hot, axis=0) - one_hot) * one_hot, axis=1)
    dest = target * capacity + slot
    slots = experts * capacity
    hit = (dest[:, None] == jnp.arange(slots, dtype=jnp.int32)[None, :]).reshape(
        tok_rows, top_count, slots
    )
    flat_scores = route_scores.reshape(tok_rows, top_count)
    combine = jnp.sum(jnp.where(hit, flat_scores[:, :, None], 0.0), axis=1)
    pick = jnp.any(hit, axis=1).astype(jnp.bfloat16)
    outgoing = matmul(pick.T, normed).astype(jnp.bfloat16)
    arrived = exchange(outgoing.reshape(experts, capacity, block_width), "dp", 5)
    arrived = arrived.reshape(slots, block_width)
    copies = jnp.broadcast_to(arrived[None], (mp_count, slots, block_width))
    in_rows = lax.all_to_all(copies, "mp", split_axis=0, concat_axis=0, tiled=True)
    gate_block = expert_gate[0].reshape(mp_count, block_width, -1)
    up_block = expert_up[0].reshape(mp_count, block_width, -1)
    gate_val = jnp.einsum("qsf,qfh->sh", in_rows, gate_block, preferred_element_type=jnp.float32)
    up_val = jnp.einsum("qsf,qfh->sh", in_rows, up_block, preferred_element_type=jnp.float32)
    activated = (jax.nn.silu(gate_val) * up_val).astype(jnp.bfloat16)
    down_block = expert_down[0].reshape(-1, mp_count, block_width)
    partial_out = jnp.einsum(
        "sh,hqf->qsf", activated, down_block, preferred_element_type=jnp.float32
    ).astype(jnp.bfloat16)
    summed = lax.all_to_all(partial_out, "mp", split_axis=0, concat_axis=0, tiled=True)
    expert_out = jnp.sum(summed.astype(jnp.float32), axis=0).astype(jnp.bfloat16)
    returned = lax.all_to_all(
        expert_out.reshape(experts, capacity, block_width),
        dp,
        split_axis=0,
        concat_axis=0,
        tiled=True,
    ).reshape(slots, block_width)
    routed = jnp.dot(
        combine,
        returned.astype(jnp.float32),
        precision=lax.Precision.HIGHEST,
        preferred_element_type=jnp.float32,
    )

    hidden_units = shared_gate.shape[1]
    shared_all = lax.all_gather(
        jnp.concatenate([shared_gate, shared_up, shared_down.T], axis=1), dp, axis=0, tiled=True
    )
    shared_gval = matmul(whole_rows, shared_all[:, :hidden_units])
    shared_uval = matmul(whole_rows, shared_all[:, hidden_units : 2 * hidden_units])
    shared_act = (jax.nn.silu(shared_gval) * shared_uval).astype(jnp.bfloat16)
    shared_part = jnp.einsum(
        "th,qfh->qtf",
        shared_act,
        shared_all[:, 2 * hidden_units :].reshape(mp_count, block_width, hidden_units),
        preferred_element_type=jnp.float32,
    )
    mixture = reduce_scatter_mp(shared_part, 4) + routed
    final = (hidden_float + mixture).astype(jnp.bfloat16)
    final_float = final.astype(jnp.float32)
    own_squares = jnp.sum(final_float * final_float, axis=1)
    square_rows = jnp.broadcast_to(own_squares[None, :], (8, tok_rows))
    final_squares = jnp.sum(
        gather_rows(square_rows, "mp", 2).reshape(mp_count, 8, tok_rows)[:, 0, :], axis=0
    )
    next_normed = (
        final_float * lax.rsqrt(final_squares / model_width + EPSILON)[:, None] * next_gain
    ).astype(jnp.bfloat16)
    return (final, next_normed)


def solution(mesh):
    dp_count, mp_count = mesh.devices.shape
    paired = Mesh(mesh.devices.reshape(dp_count // 2, 2, mp_count), ("g", "c", "mp"))
    dp = ("g", "c")
    in_specs = (
        P(dp, "mp"),
        P(dp, "mp"),
        P("mp", dp),
        P("mp"),
        P(dp, "mp"),
        P(dp, "mp"),
        P("mp", dp),
        P(dp, None, "mp"),
        P(dp, None, "mp"),
        P(dp, "mp", None),
        P(dp, None),
        P(dp, None),
        P(),
        P("mp"),
    )
    out_specs = (P(dp, "mp"), P(dp, "mp"))
    return jax.shard_map(local, mesh=paired, in_specs=in_specs, out_specs=out_specs, check_vma=False)
```

```python
import functools

import jax
import jax.numpy as jnp
from jax import lax
from jax.experimental import pallas as pl
from jax.experimental.pallas import tpu as pltpu
from jax.sharding import Mesh, PartitionSpec as P

MESH = pl.DeviceIdType.MESH

D = 2048


EPSILON = 1e-06


def matmul(left, right):
    return jnp.dot(left, right, preferred_element_type=jnp.float32)


def matmul_t(left, right_t):
    return lax.dot_general(
        left, right_t, (((1,), (1,)), ((), ())), preferred_element_type=jnp.float32
    )


def _gather_kernel(axis, x_ref, o_ref, send_sem, recv_sem):
    coords = {name: lax.axis_index(name) for name in ("g", "c", "mp")}
    n = lax.axis_size(axis)
    me = coords[axis]
    rows = x_ref.shape[0]

    def device(peer):
        return tuple(peer if name == axis else coords[name] for name in ("g", "c", "mp"))

    barrier = pltpu.get_barrier_semaphore()

    def greet(p, carry):
        peer = lax.rem(me + p, n)
        pl.semaphore_signal(barrier, inc=1, device_id=device(peer), device_id_type=MESH)
        return carry

    lax.fori_loop(1, n, greet, 0)
    pl.semaphore_wait(barrier, n - 1)
    own = o_ref.at[pl.ds(me * rows, rows)]
    pltpu.make_async_copy(x_ref, own, recv_sem).start()

    def send(p, carry):
        peer = lax.rem(me + p, n)
        pltpu.make_async_remote_copy(
            src_ref=x_ref,
            dst_ref=own,
            send_sem=send_sem,
            recv_sem=recv_sem,
            device_id=device(peer),
            device_id_type=MESH,
        ).start()
        return carry

    lax.fori_loop(1, n, send, 0)
    sent = o_ref.at[pl.ds(0, (n - 1) * rows)]
    pltpu.make_async_copy(sent, sent, send_sem).wait()
    pltpu.make_async_copy(o_ref, o_ref, recv_sem).wait()


def gather_rows(x, axis, collective_id):
    n = lax.axis_size(axis)
    rows, cols = x.shape
    return pl.pallas_call(
        functools.partial(_gather_kernel, axis),
        out_shape=jax.ShapeDtypeStruct((n * rows, cols), x.dtype),
        in_specs=[pl.BlockSpec(memory_space=pl.ANY)],
        out_specs=pl.BlockSpec(memory_space=pl.ANY),
        scratch_shapes=[pltpu.SemaphoreType.DMA(()), pltpu.SemaphoreType.DMA(())],
        compiler_params=pltpu.CompilerParams(collective_id=collective_id, has_side_effects=True),
    )(x)


def _exchange_kernel(axis, x_ref, o_ref, send_sem, recv_sem):
    coords = {name: lax.axis_index(name) for name in ("g", "c", "mp")}
    if axis == "dp":
        cores = lax.axis_size("c")
        n = lax.axis_size("g") * cores
        me = coords["g"] * cores + coords["c"]

        def device(peer):
            return (peer // cores, peer % cores, coords["mp"])

    else:
        n = lax.axis_size(axis)
        me = coords[axis]

        def device(peer):
            return tuple(peer if name == axis else coords[name] for name in ("g", "c", "mp"))

    barrier = pltpu.get_barrier_semaphore()

    def greet(p, carry):
        peer = lax.rem(me + p, n)
        pl.semaphore_signal(barrier, inc=1, device_id=device(peer), device_id_type=MESH)
        return carry

    lax.fori_loop(1, n, greet, 0)
    pl.semaphore_wait(barrier, n - 1)
    pltpu.make_async_copy(x_ref.at[me], o_ref.at[me], recv_sem).start()

    def send(p, carry):
        peer = lax.rem(me + p, n)
        pltpu.make_async_remote_copy(
            src_ref=x_ref.at[peer],
            dst_ref=o_ref.at[me],
            send_sem=send_sem,
            recv_sem=recv_sem,
            device_id=device(peer),
            device_id_type=MESH,
        ).start()
        return carry

    lax.fori_loop(1, n, send, 0)
    sent = o_ref.at[pl.ds(0, n - 1)]
    pltpu.make_async_copy(sent, sent, send_sem).wait()
    pltpu.make_async_copy(o_ref, o_ref, recv_sem).wait()


def exchange(x, axis, collective_id):
    return pl.pallas_call(
        functools.partial(_exchange_kernel, axis),
        out_shape=jax.ShapeDtypeStruct(x.shape, x.dtype),
        in_specs=[pl.BlockSpec(memory_space=pl.ANY)],
        out_specs=pl.BlockSpec(memory_space=pl.ANY),
        scratch_shapes=[pltpu.SemaphoreType.DMA(()), pltpu.SemaphoreType.DMA(())],
        compiler_params=pltpu.CompilerParams(collective_id=collective_id, has_side_effects=True),
    )(x)


def reduce_scatter_mp(blocks, collective_id):
    return jnp.sum(exchange(blocks, "mp", collective_id), axis=0)


def swap_halves(value, tok_rows):
    return lax.all_to_all(
        value.reshape(2, tok_rows, value.shape[1]), "c", split_axis=0, concat_axis=0, tiled=True
    )


def natural_blocks(halves, mp_count):
    _, rows, cols = halves.shape
    pairs = lax.axis_size("g")
    width = cols // pairs
    ordered = jnp.transpose(halves.reshape(2, rows, pairs, width), (1, 2, 0, 3))
    return jnp.transpose(ordered.reshape(rows, mp_count, -1), (1, 0, 2))


def local(
    attention,
    residual,
    out_weight,
    ffn_gain,
    shared_gate,
    shared_up,
    shared_down,
    expert_gate,
    expert_up,
    expert_down,
    route_ids,
    route_scores,
    placement,
    next_gain,
):
    dp = ("g", "c")
    tok_rows = attention.shape[0]
    top_count = route_ids.shape[1]
    mp_count = lax.axis_size("mp")
    pairs = lax.axis_size("g")
    experts = pairs * lax.axis_size("c")
    core = lax.axis_index("c")
    capacity = min(tok_rows, 8 * tok_rows // experts)
    model_width = D
    block_width = model_width // mp_count

    w_half = gather_rows(out_weight.T, "g", 0)
    att_pair = lax.all_gather(attention, "c", axis=0, tiled=True)
    part_half = matmul_t(att_pair, w_half)
    partial_value = natural_blocks(swap_halves(part_half, tok_rows), mp_count)
    gain_row = jnp.broadcast_to(ffn_gain[None, None, :], (mp_count, 1, block_width))
    exchanged = exchange(jnp.concatenate([partial_value, gain_row], axis=1), "mp", 3)
    projected = jnp.sum(exchanged[:, :tok_rows, :], axis=0)
    gain = exchanged[:, tok_rows, :].reshape(model_width)
    hidden = (residual.astype(jnp.float32) + projected).astype(jnp.bfloat16)
    hidden_float = hidden.astype(jnp.float32)
    hidden_blocks = gather_rows(hidden, "mp", 1).reshape(mp_count, tok_rows, block_width)
    whole_hidden = jnp.transpose(hidden_blocks, (1, 0, 2)).reshape(tok_rows, model_width)
    whole_hidden = whole_hidden.astype(jnp.float32)
    squares = jnp.sum(whole_hidden * whole_hidden, axis=1)
    scale = lax.rsqrt(squares / model_width + EPSILON)[:, None]
    whole_rows = (whole_hidden * scale * gain).astype(jnp.bfloat16)
    normed = (hidden_float * scale * ffn_gain).astype(jnp.bfloat16)

    flat_ids = route_ids.reshape(-1)
    expert_iota = jnp.arange(experts, dtype=jnp.int32)
    one_hot = (flat_ids[:, None] == expert_iota[None, :]).astype(jnp.int32)
    target = jnp.sum(one_hot * placement[None, :], axis=1)
    slot = jnp.sum((jnp.cumsum(one_hot, axis=0) - one_hot) * one_hot, axis=1)
    dest = target * capacity + slot
    slots = experts * capacity
    hit = (dest[:, None] == jnp.arange(slots, dtype=jnp.int32)[None, :]).reshape(
        tok_rows, top_count, slots
    )
    flat_scores = route_scores.reshape(tok_rows, top_count)
    combine = jnp.sum(jnp.where(hit, flat_scores[:, :, None], 0.0), axis=1)
    pick = jnp.any(hit, axis=1).astype(jnp.bfloat16)
    half = block_width // 2
    gate_block = expert_gate[0].reshape(mp_count, block_width, -1)
    up_block = expert_up[0].reshape(mp_count, block_width, -1)
    gate_val = None
    up_val = None
    for part in range(2):
        columns = slice(part * half, (part + 1) * half)
        outgoing = matmul(pick.T, normed[:, columns]).astype(jnp.bfloat16)
        arrived = exchange(outgoing.reshape(experts, capacity, half), "dp", 5 + part)
        copies = jnp.broadcast_to(arrived.reshape(1, slots, half), (mp_count, slots, half))
        in_rows = lax.all_to_all(copies, "mp", split_axis=0, concat_axis=0, tiled=True)
        gate_part = jnp.einsum(
            "qsf,qfh->sh", in_rows, gate_block[:, columns, :], preferred_element_type=jnp.float32
        )
        up_part = jnp.einsum(
            "qsf,qfh->sh", in_rows, up_block[:, columns, :], preferred_element_type=jnp.float32
        )
        gate_val = gate_part if gate_val is None else gate_val + gate_part
        up_val = up_part if up_val is None else up_val + up_part
    activated = (jax.nn.silu(gate_val) * up_val).astype(jnp.bfloat16)
    down_block = expert_down[0].reshape(-1, mp_count, block_width)
    partial_out = jnp.einsum(
        "sh,hqf->qsf", activated, down_block, preferred_element_type=jnp.float32
    ).astype(jnp.bfloat16)
    summed = lax.all_to_all(partial_out, "mp", split_axis=0, concat_axis=0, tiled=True)
    expert_out = jnp.sum(summed.astype(jnp.float32), axis=0).astype(jnp.bfloat16)
    returned = lax.all_to_all(
        expert_out.reshape(experts, capacity, block_width),
        dp,
        split_axis=0,
        concat_axis=0,
        tiled=True,
    ).reshape(slots, block_width)
    routed = jnp.dot(
        combine,
        returned.astype(jnp.float32),
        precision=lax.Precision.HIGHEST,
        preferred_element_type=jnp.float32,
    )

    hidden_units = shared_gate.shape[1]
    shared_all = lax.all_gather(
        jnp.concatenate([shared_gate, shared_up, shared_down.T], axis=1), dp, axis=0, tiled=True
    )
    shared_gval = matmul(whole_rows, shared_all[:, :hidden_units])
    shared_uval = matmul(whole_rows, shared_all[:, hidden_units : 2 * hidden_units])
    shared_act = (jax.nn.silu(shared_gval) * shared_uval).astype(jnp.bfloat16)
    shared_part = jnp.einsum(
        "th,qfh->qtf",
        shared_act,
        shared_all[:, 2 * hidden_units :].reshape(mp_count, block_width, hidden_units),
        preferred_element_type=jnp.float32,
    )
    mixture = reduce_scatter_mp(shared_part, 4) + routed
    final = (hidden_float + mixture).astype(jnp.bfloat16)
    final_float = final.astype(jnp.float32)
    own_squares = jnp.sum(final_float * final_float, axis=1)
    square_rows = jnp.broadcast_to(own_squares[None, :], (8, tok_rows))
    final_squares = jnp.sum(
        gather_rows(square_rows, "mp", 2).reshape(mp_count, 8, tok_rows)[:, 0, :], axis=0
    )
    next_normed = (
        final_float * lax.rsqrt(final_squares / model_width + EPSILON)[:, None] * next_gain
    ).astype(jnp.bfloat16)
    return (final, next_normed)


def solution(mesh):
    dp_count, mp_count = mesh.devices.shape
    paired = Mesh(mesh.devices.reshape(dp_count // 2, 2, mp_count), ("g", "c", "mp"))
    dp = ("g", "c")
    in_specs = (
        P(dp, "mp"),
        P(dp, "mp"),
        P("mp", dp),
        P("mp"),
        P(dp, "mp"),
        P(dp, "mp"),
        P("mp", dp),
        P(dp, None, "mp"),
        P(dp, None, "mp"),
        P(dp, "mp", None),
        P(dp, None),
        P(dp, None),
        P(),
        P("mp"),
    )
    out_specs = (P(dp, "mp"), P(dp, "mp"))
    return jax.shard_map(local, mesh=paired, in_specs=in_specs, out_specs=out_specs, check_vma=False)
```

```python
import functools

import jax
import jax.numpy as jnp
from jax import lax
from jax.experimental import pallas as pl
from jax.experimental.pallas import tpu as pltpu
from jax.sharding import Mesh, PartitionSpec as P

MESH = pl.DeviceIdType.MESH

D = 2048


EPSILON = 1e-06


def matmul(left, right):
    return jnp.dot(left, right, preferred_element_type=jnp.float32)


def matmul_t(left, right_t):
    return lax.dot_general(
        left, right_t, (((1,), (1,)), ((), ())), preferred_element_type=jnp.float32
    )


def _gather_kernel(axis, x_ref, o_ref, send_sem, recv_sem):
    coords = {name: lax.axis_index(name) for name in ("g", "c", "mp")}
    n = lax.axis_size(axis)
    me = coords[axis]
    rows = x_ref.shape[0]

    def device(peer):
        return tuple(peer if name == axis else coords[name] for name in ("g", "c", "mp"))

    barrier = pltpu.get_barrier_semaphore()

    def greet(p, carry):
        peer = lax.rem(me + p, n)
        pl.semaphore_signal(barrier, inc=1, device_id=device(peer), device_id_type=MESH)
        return carry

    lax.fori_loop(1, n, greet, 0)
    pl.semaphore_wait(barrier, n - 1)
    own = o_ref.at[pl.ds(me * rows, rows)]
    pltpu.make_async_copy(x_ref, own, recv_sem).start()

    def send(p, carry):
        peer = lax.rem(me + p, n)
        pltpu.make_async_remote_copy(
            src_ref=x_ref,
            dst_ref=own,
            send_sem=send_sem,
            recv_sem=recv_sem,
            device_id=device(peer),
            device_id_type=MESH,
        ).start()
        return carry

    lax.fori_loop(1, n, send, 0)
    sent = o_ref.at[pl.ds(0, (n - 1) * rows)]
    pltpu.make_async_copy(sent, sent, send_sem).wait()
    pltpu.make_async_copy(o_ref, o_ref, recv_sem).wait()


def gather_rows(x, axis, collective_id):
    n = lax.axis_size(axis)
    rows, cols = x.shape
    return pl.pallas_call(
        functools.partial(_gather_kernel, axis),
        out_shape=jax.ShapeDtypeStruct((n * rows, cols), x.dtype),
        in_specs=[pl.BlockSpec(memory_space=pl.ANY)],
        out_specs=pl.BlockSpec(memory_space=pl.ANY),
        scratch_shapes=[pltpu.SemaphoreType.DMA(()), pltpu.SemaphoreType.DMA(())],
        compiler_params=pltpu.CompilerParams(collective_id=collective_id, has_side_effects=True),
    )(x)


def _exchange_kernel(axis, x_ref, o_ref, send_sem, recv_sem):
    coords = {name: lax.axis_index(name) for name in ("g", "c", "mp")}
    if axis == "dp":
        cores = lax.axis_size("c")
        n = lax.axis_size("g") * cores
        me = coords["g"] * cores + coords["c"]

        def device(peer):
            return (peer // cores, peer % cores, coords["mp"])

    else:
        n = lax.axis_size(axis)
        me = coords[axis]

        def device(peer):
            return tuple(peer if name == axis else coords[name] for name in ("g", "c", "mp"))

    barrier = pltpu.get_barrier_semaphore()

    def greet(p, carry):
        peer = lax.rem(me + p, n)
        pl.semaphore_signal(barrier, inc=1, device_id=device(peer), device_id_type=MESH)
        return carry

    lax.fori_loop(1, n, greet, 0)
    pl.semaphore_wait(barrier, n - 1)
    pltpu.make_async_copy(x_ref.at[me], o_ref.at[me], recv_sem).start()

    def send(p, carry):
        peer = lax.rem(me + p, n)
        pltpu.make_async_remote_copy(
            src_ref=x_ref.at[peer],
            dst_ref=o_ref.at[me],
            send_sem=send_sem,
            recv_sem=recv_sem,
            device_id=device(peer),
            device_id_type=MESH,
        ).start()
        return carry

    lax.fori_loop(1, n, send, 0)
    sent = o_ref.at[pl.ds(0, n - 1)]
    pltpu.make_async_copy(sent, sent, send_sem).wait()
    pltpu.make_async_copy(o_ref, o_ref, recv_sem).wait()


def exchange(x, axis, collective_id):
    return pl.pallas_call(
        functools.partial(_exchange_kernel, axis),
        out_shape=jax.ShapeDtypeStruct(x.shape, x.dtype),
        in_specs=[pl.BlockSpec(memory_space=pl.ANY)],
        out_specs=pl.BlockSpec(memory_space=pl.ANY),
        scratch_shapes=[pltpu.SemaphoreType.DMA(()), pltpu.SemaphoreType.DMA(())],
        compiler_params=pltpu.CompilerParams(collective_id=collective_id, has_side_effects=True),
    )(x)


def reduce_scatter_mp(blocks, collective_id):
    return jnp.sum(exchange(blocks, "mp", collective_id), axis=0)


def swap_halves(value, tok_rows):
    return lax.all_to_all(
        value.reshape(2, tok_rows, value.shape[1]), "c", split_axis=0, concat_axis=0, tiled=True
    )


def natural_blocks(halves, mp_count):
    _, rows, cols = halves.shape
    pairs = lax.axis_size("g")
    width = cols // pairs
    ordered = jnp.transpose(halves.reshape(2, rows, pairs, width), (1, 2, 0, 3))
    return jnp.transpose(ordered.reshape(rows, mp_count, -1), (1, 0, 2))


def local(
    attention,
    residual,
    out_weight,
    ffn_gain,
    shared_gate,
    shared_up,
    shared_down,
    expert_gate,
    expert_up,
    expert_down,
    route_ids,
    route_scores,
    placement,
    next_gain,
):
    dp = ("g", "c")
    tok_rows = attention.shape[0]
    top_count = route_ids.shape[1]
    mp_count = lax.axis_size("mp")
    pairs = lax.axis_size("g")
    experts = pairs * lax.axis_size("c")
    core = lax.axis_index("c")
    capacity = min(tok_rows, 8 * tok_rows // experts)
    model_width = D
    block_width = model_width // mp_count

    w_half = gather_rows(out_weight.T, "g", 0)
    att_pair = lax.all_gather(attention, "c", axis=0, tiled=True)
    part_half = matmul_t(att_pair, w_half)
    partial_value = natural_blocks(swap_halves(part_half, tok_rows), mp_count)
    gain_row = jnp.broadcast_to(ffn_gain[None, None, :], (mp_count, 1, block_width))
    exchanged = exchange(jnp.concatenate([partial_value, gain_row], axis=1), "mp", 3)
    projected = jnp.sum(exchanged[:, :tok_rows, :], axis=0)
    gain = exchanged[:, tok_rows, :].reshape(model_width)
    hidden = (residual.astype(jnp.float32) + projected).astype(jnp.bfloat16)
    hidden_float = hidden.astype(jnp.float32)
    hidden_blocks = gather_rows(hidden, "mp", 1).reshape(mp_count, tok_rows, block_width)
    whole_hidden = jnp.transpose(hidden_blocks, (1, 0, 2)).reshape(tok_rows, model_width)
    whole_hidden = whole_hidden.astype(jnp.float32)
    squares = jnp.sum(whole_hidden * whole_hidden, axis=1)
    scale = lax.rsqrt(squares / model_width + EPSILON)[:, None]
    whole_rows = (whole_hidden * scale * gain).astype(jnp.bfloat16)
    normed = (hidden_float * scale * ffn_gain).astype(jnp.bfloat16)

    flat_ids = route_ids.reshape(-1)
    expert_iota = jnp.arange(experts, dtype=jnp.int32)
    one_hot = (flat_ids[:, None] == expert_iota[None, :]).astype(jnp.int32)
    target = jnp.sum(one_hot * placement[None, :], axis=1)
    slot = jnp.sum((jnp.cumsum(one_hot, axis=0) - one_hot) * one_hot, axis=1)
    dest = target * capacity + slot
    slots = experts * capacity
    hit = (dest[:, None] == jnp.arange(slots, dtype=jnp.int32)[None, :]).reshape(
        tok_rows, top_count, slots
    )
    flat_scores = route_scores.reshape(tok_rows, top_count)
    combine = jnp.sum(jnp.where(hit, flat_scores[:, :, None], 0.0), axis=1)
    pick = jnp.any(hit, axis=1).astype(jnp.bfloat16)
    hidden_units = shared_gate.shape[1]
    shared_all = lax.all_gather(
        jnp.concatenate([shared_gate, shared_up, shared_down.T], axis=1), dp, axis=0, tiled=True
    )
    shared_gval = matmul(whole_rows, shared_all[:, :hidden_units])
    shared_uval = matmul(whole_rows, shared_all[:, hidden_units : 2 * hidden_units])
    shared_act = (jax.nn.silu(shared_gval) * shared_uval).astype(jnp.bfloat16)
    shared_part = jnp.einsum(
        "th,qfh->qtf",
        shared_act,
        shared_all[:, 2 * hidden_units :].reshape(mp_count, block_width, hidden_units),
        preferred_element_type=jnp.float32,
    )
    half = block_width // 2
    gate_block = expert_gate[0].reshape(mp_count, block_width, -1)
    up_block = expert_up[0].reshape(mp_count, block_width, -1)
    gate_val = None
    up_val = None
    for part in range(2):
        columns = slice(part * half, (part + 1) * half)
        outgoing = matmul(pick.T, normed[:, columns]).astype(jnp.bfloat16)
        arrived = exchange(outgoing.reshape(experts, capacity, half), "dp", 5 + part)
        copies = jnp.broadcast_to(arrived.reshape(1, slots, half), (mp_count, slots, half))
        in_rows = lax.all_to_all(copies, "mp", split_axis=0, concat_axis=0, tiled=True)
        if part == 1:
            in_rows, shared_part = lax.optimization_barrier((in_rows, shared_part))
        gate_part = jnp.einsum(
            "qsf,qfh->sh", in_rows, gate_block[:, columns, :], preferred_element_type=jnp.float32
        )
        up_part = jnp.einsum(
            "qsf,qfh->sh", in_rows, up_block[:, columns, :], preferred_element_type=jnp.float32
        )
        gate_val = gate_part if gate_val is None else gate_val + gate_part
        up_val = up_part if up_val is None else up_val + up_part
    activated = (jax.nn.silu(gate_val) * up_val).astype(jnp.bfloat16)
    down_block = expert_down[0].reshape(-1, mp_count, block_width)
    partial_out = jnp.einsum(
        "sh,hqf->qsf", activated, down_block, preferred_element_type=jnp.float32
    ).astype(jnp.bfloat16)
    summed = lax.all_to_all(partial_out, "mp", split_axis=0, concat_axis=0, tiled=True)
    expert_out = jnp.sum(summed.astype(jnp.float32), axis=0).astype(jnp.bfloat16)
    returned = lax.all_to_all(
        expert_out.reshape(experts, capacity, block_width),
        dp,
        split_axis=0,
        concat_axis=0,
        tiled=True,
    ).reshape(slots, block_width)
    routed = jnp.dot(
        combine,
        returned.astype(jnp.float32),
        precision=lax.Precision.HIGHEST,
        preferred_element_type=jnp.float32,
    )

    mixture = reduce_scatter_mp(shared_part, 4) + routed
    final = (hidden_float + mixture).astype(jnp.bfloat16)
    final_float = final.astype(jnp.float32)
    own_squares = jnp.sum(final_float * final_float, axis=1)
    square_rows = jnp.broadcast_to(own_squares[None, :], (8, tok_rows))
    final_squares = jnp.sum(
        gather_rows(square_rows, "mp", 2).reshape(mp_count, 8, tok_rows)[:, 0, :], axis=0
    )
    next_normed = (
        final_float * lax.rsqrt(final_squares / model_width + EPSILON)[:, None] * next_gain
    ).astype(jnp.bfloat16)
    return (final, next_normed)


def solution(mesh):
    dp_count, mp_count = mesh.devices.shape
    paired = Mesh(mesh.devices.reshape(dp_count // 2, 2, mp_count), ("g", "c", "mp"))
    dp = ("g", "c")
    in_specs = (
        P(dp, "mp"),
        P(dp, "mp"),
        P("mp", dp),
        P("mp"),
        P(dp, "mp"),
        P(dp, "mp"),
        P("mp", dp),
        P(dp, None, "mp"),
        P(dp, None, "mp"),
        P(dp, "mp", None),
        P(dp, None),
        P(dp, None),
        P(),
        P("mp"),
    )
    out_specs = (P(dp, "mp"), P(dp, "mp"))
    return jax.shard_map(local, mesh=paired, in_specs=in_specs, out_specs=out_specs, check_vma=False)
```

```python
import functools

import jax
import jax.numpy as jnp
from jax import lax
from jax.experimental import pallas as pl
from jax.experimental.pallas import tpu as pltpu
from jax.sharding import Mesh, PartitionSpec as P

MESH = pl.DeviceIdType.MESH

D = 2048


EPSILON = 1e-06


def matmul(left, right):
    return jnp.dot(left, right, preferred_element_type=jnp.float32)


def matmul_t(left, right_t):
    return lax.dot_general(
        left, right_t, (((1,), (1,)), ((), ())), preferred_element_type=jnp.float32
    )


def _gather_kernel(axis, x_ref, o_ref, send_sem, recv_sem):
    coords = {name: lax.axis_index(name) for name in ("g", "c", "mp")}
    n = lax.axis_size(axis)
    me = coords[axis]
    rows = x_ref.shape[0]

    def device(peer):
        return tuple(peer if name == axis else coords[name] for name in ("g", "c", "mp"))

    barrier = pltpu.get_barrier_semaphore()

    def greet(p, carry):
        peer = lax.rem(me + p, n)
        pl.semaphore_signal(barrier, inc=1, device_id=device(peer), device_id_type=MESH)
        return carry

    lax.fori_loop(1, n, greet, 0)
    pl.semaphore_wait(barrier, n - 1)
    own = o_ref.at[pl.ds(me * rows, rows)]
    pltpu.make_async_copy(x_ref, own, recv_sem).start()

    def send(p, carry):
        peer = lax.rem(me + p, n)
        pltpu.make_async_remote_copy(
            src_ref=x_ref,
            dst_ref=own,
            send_sem=send_sem,
            recv_sem=recv_sem,
            device_id=device(peer),
            device_id_type=MESH,
        ).start()
        return carry

    lax.fori_loop(1, n, send, 0)
    sent = o_ref.at[pl.ds(0, (n - 1) * rows)]
    pltpu.make_async_copy(sent, sent, send_sem).wait()
    pltpu.make_async_copy(o_ref, o_ref, recv_sem).wait()


def gather_rows(x, axis, collective_id):
    n = lax.axis_size(axis)
    rows, cols = x.shape
    return pl.pallas_call(
        functools.partial(_gather_kernel, axis),
        out_shape=jax.ShapeDtypeStruct((n * rows, cols), x.dtype),
        in_specs=[pl.BlockSpec(memory_space=pl.ANY)],
        out_specs=pl.BlockSpec(memory_space=pl.ANY),
        scratch_shapes=[pltpu.SemaphoreType.DMA(()), pltpu.SemaphoreType.DMA(())],
        compiler_params=pltpu.CompilerParams(collective_id=collective_id, has_side_effects=True),
    )(x)


def _exchange_kernel(axis, x_ref, o_ref, send_sem, recv_sem):
    coords = {name: lax.axis_index(name) for name in ("g", "c", "mp")}
    if axis == "dp":
        cores = lax.axis_size("c")
        n = lax.axis_size("g") * cores
        me = coords["g"] * cores + coords["c"]

        def device(peer):
            return (peer // cores, peer % cores, coords["mp"])

    else:
        n = lax.axis_size(axis)
        me = coords[axis]

        def device(peer):
            return tuple(peer if name == axis else coords[name] for name in ("g", "c", "mp"))

    barrier = pltpu.get_barrier_semaphore()

    def greet(p, carry):
        peer = lax.rem(me + p, n)
        pl.semaphore_signal(barrier, inc=1, device_id=device(peer), device_id_type=MESH)
        return carry

    lax.fori_loop(1, n, greet, 0)
    pl.semaphore_wait(barrier, n - 1)
    pltpu.make_async_copy(x_ref.at[me], o_ref.at[me], recv_sem).start()

    def send(p, carry):
        peer = lax.rem(me + p, n)
        pltpu.make_async_remote_copy(
            src_ref=x_ref.at[peer],
            dst_ref=o_ref.at[me],
            send_sem=send_sem,
            recv_sem=recv_sem,
            device_id=device(peer),
            device_id_type=MESH,
        ).start()
        return carry

    lax.fori_loop(1, n, send, 0)
    sent = o_ref.at[pl.ds(0, n - 1)]
    pltpu.make_async_copy(sent, sent, send_sem).wait()
    pltpu.make_async_copy(o_ref, o_ref, recv_sem).wait()


def exchange(x, axis, collective_id):
    return pl.pallas_call(
        functools.partial(_exchange_kernel, axis),
        out_shape=jax.ShapeDtypeStruct(x.shape, x.dtype),
        in_specs=[pl.BlockSpec(memory_space=pl.ANY)],
        out_specs=pl.BlockSpec(memory_space=pl.ANY),
        scratch_shapes=[pltpu.SemaphoreType.DMA(()), pltpu.SemaphoreType.DMA(())],
        compiler_params=pltpu.CompilerParams(collective_id=collective_id, has_side_effects=True),
    )(x)


def reduce_scatter_mp(blocks, collective_id):
    return jnp.sum(exchange(blocks, "mp", collective_id), axis=0)


def swap_halves(value, tok_rows):
    return lax.all_to_all(
        value.reshape(2, tok_rows, value.shape[1]), "c", split_axis=0, concat_axis=0, tiled=True
    )


def natural_blocks(halves, mp_count):
    _, rows, cols = halves.shape
    pairs = lax.axis_size("g")
    width = cols // pairs
    ordered = jnp.transpose(halves.reshape(2, rows, pairs, width), (1, 2, 0, 3))
    return jnp.transpose(ordered.reshape(rows, mp_count, -1), (1, 0, 2))


def local(
    attention,
    residual,
    out_weight,
    ffn_gain,
    shared_gate,
    shared_up,
    shared_down,
    expert_gate,
    expert_up,
    expert_down,
    route_ids,
    route_scores,
    placement,
    next_gain,
):
    dp = ("g", "c")
    tok_rows = attention.shape[0]
    top_count = route_ids.shape[1]
    mp_count = lax.axis_size("mp")
    pairs = lax.axis_size("g")
    experts = pairs * lax.axis_size("c")
    core = lax.axis_index("c")
    capacity = min(tok_rows, 8 * tok_rows // experts)
    model_width = D
    block_width = model_width // mp_count

    w_half = gather_rows(out_weight.T, "g", 0)
    att_pair = lax.all_gather(attention, "c", axis=0, tiled=True)
    part_half = matmul_t(att_pair, w_half)
    partial_value = natural_blocks(swap_halves(part_half, tok_rows), mp_count)
    gain_row = jnp.broadcast_to(ffn_gain[None, None, :], (mp_count, 1, block_width))
    exchanged = exchange(jnp.concatenate([partial_value, gain_row], axis=1), "mp", 3)
    projected = jnp.sum(exchanged[:, :tok_rows, :], axis=0)
    gain = exchanged[:, tok_rows, :].reshape(model_width)
    hidden = (residual.astype(jnp.float32) + projected).astype(jnp.bfloat16)
    hidden_float = hidden.astype(jnp.float32)
    hidden_blocks = gather_rows(hidden, "mp", 1).reshape(mp_count, tok_rows, block_width)
    whole_hidden = jnp.transpose(hidden_blocks, (1, 0, 2)).reshape(tok_rows, model_width)
    whole_hidden = whole_hidden.astype(jnp.float32)
    squares = jnp.sum(whole_hidden * whole_hidden, axis=1)
    scale = lax.rsqrt(squares / model_width + EPSILON)[:, None]
    whole_rows = (whole_hidden * scale * gain).astype(jnp.bfloat16)
    normed = (hidden_float * scale * ffn_gain).astype(jnp.bfloat16)

    flat_ids = route_ids.reshape(-1)
    expert_iota = jnp.arange(experts, dtype=jnp.int32)
    one_hot = (flat_ids[:, None] == expert_iota[None, :]).astype(jnp.int32)
    target = jnp.sum(one_hot * placement[None, :], axis=1)
    slot = jnp.sum((jnp.cumsum(one_hot, axis=0) - one_hot) * one_hot, axis=1)
    dest = target * capacity + slot
    slots = experts * capacity
    hit = (dest[:, None] == jnp.arange(slots, dtype=jnp.int32)[None, :]).reshape(
        tok_rows, top_count, slots
    )
    flat_scores = route_scores.reshape(tok_rows, top_count)
    combine = jnp.sum(jnp.where(hit, flat_scores[:, :, None], 0.0), axis=1)
    pick = jnp.any(hit, axis=1).astype(jnp.bfloat16)
    chunks = 4
    half = block_width // chunks
    gate_block = expert_gate[0].reshape(mp_count, block_width, -1)
    up_block = expert_up[0].reshape(mp_count, block_width, -1)
    gate_val = None
    up_val = None
    for part in range(chunks):
        columns = slice(part * half, (part + 1) * half)
        outgoing = matmul(pick.T, normed[:, columns]).astype(jnp.bfloat16)
        arrived = exchange(outgoing.reshape(experts, capacity, half), "dp", 5 + part)
        copies = jnp.broadcast_to(arrived.reshape(1, slots, half), (mp_count, slots, half))
        in_rows = lax.all_to_all(copies, "mp", split_axis=0, concat_axis=0, tiled=True)
        gate_part = jnp.einsum(
            "qsf,qfh->sh", in_rows, gate_block[:, columns, :], preferred_element_type=jnp.float32
        )
        up_part = jnp.einsum(
            "qsf,qfh->sh", in_rows, up_block[:, columns, :], preferred_element_type=jnp.float32
        )
        gate_val = gate_part if gate_val is None else gate_val + gate_part
        up_val = up_part if up_val is None else up_val + up_part
    activated = (jax.nn.silu(gate_val) * up_val).astype(jnp.bfloat16)
    down_block = expert_down[0].reshape(-1, mp_count, block_width)
    partial_out = jnp.einsum(
        "sh,hqf->qsf", activated, down_block, preferred_element_type=jnp.float32
    ).astype(jnp.bfloat16)
    summed = lax.all_to_all(partial_out, "mp", split_axis=0, concat_axis=0, tiled=True)
    expert_out = jnp.sum(summed.astype(jnp.float32), axis=0).astype(jnp.bfloat16)
    returned = lax.all_to_all(
        expert_out.reshape(experts, capacity, block_width),
        dp,
        split_axis=0,
        concat_axis=0,
        tiled=True,
    ).reshape(slots, block_width)
    routed = jnp.dot(
        combine,
        returned.astype(jnp.float32),
        precision=lax.Precision.HIGHEST,
        preferred_element_type=jnp.float32,
    )

    hidden_units = shared_gate.shape[1]
    shared_all = lax.all_gather(
        jnp.concatenate([shared_gate, shared_up, shared_down.T], axis=1), dp, axis=0, tiled=True
    )
    shared_gval = matmul(whole_rows, shared_all[:, :hidden_units])
    shared_uval = matmul(whole_rows, shared_all[:, hidden_units : 2 * hidden_units])
    shared_act = (jax.nn.silu(shared_gval) * shared_uval).astype(jnp.bfloat16)
    shared_part = jnp.einsum(
        "th,qfh->qtf",
        shared_act,
        shared_all[:, 2 * hidden_units :].reshape(mp_count, block_width, hidden_units),
        preferred_element_type=jnp.float32,
    )
    mixture = reduce_scatter_mp(shared_part, 4) + routed
    final = (hidden_float + mixture).astype(jnp.bfloat16)
    final_float = final.astype(jnp.float32)
    own_squares = jnp.sum(final_float * final_float, axis=1)
    square_rows = jnp.broadcast_to(own_squares[None, :], (8, tok_rows))
    final_squares = jnp.sum(
        gather_rows(square_rows, "mp", 2).reshape(mp_count, 8, tok_rows)[:, 0, :], axis=0
    )
    next_normed = (
        final_float * lax.rsqrt(final_squares / model_width + EPSILON)[:, None] * next_gain
    ).astype(jnp.bfloat16)
    return (final, next_normed)


def solution(mesh):
    dp_count, mp_count = mesh.devices.shape
    paired = Mesh(mesh.devices.reshape(dp_count // 2, 2, mp_count), ("g", "c", "mp"))
    dp = ("g", "c")
    in_specs = (
        P(dp, "mp"),
        P(dp, "mp"),
        P("mp", dp),
        P("mp"),
        P(dp, "mp"),
        P(dp, "mp"),
        P("mp", dp),
        P(dp, None, "mp"),
        P(dp, None, "mp"),
        P(dp, "mp", None),
        P(dp, None),
        P(dp, None),
        P(),
        P("mp"),
    )
    out_specs = (P(dp, "mp"), P(dp, "mp"))
    return jax.shard_map(local, mesh=paired, in_specs=in_specs, out_specs=out_specs, check_vma=False)
```

```python
import functools

import jax
import jax.numpy as jnp
from jax import lax
from jax.experimental import pallas as pl
from jax.experimental.pallas import tpu as pltpu
from jax.sharding import Mesh, PartitionSpec as P

MESH = pl.DeviceIdType.MESH

D = 2048


EPSILON = 1e-06


def matmul(left, right):
    return jnp.dot(left, right, preferred_element_type=jnp.float32)


def matmul_t(left, right_t):
    return lax.dot_general(
        left, right_t, (((1,), (1,)), ((), ())), preferred_element_type=jnp.float32
    )


def _gather_kernel(axis, x_ref, o_ref, send_sem, recv_sem):
    coords = {name: lax.axis_index(name) for name in ("g", "c", "mp")}
    n = lax.axis_size(axis)
    me = coords[axis]
    rows = x_ref.shape[0]

    def device(peer):
        return tuple(peer if name == axis else coords[name] for name in ("g", "c", "mp"))

    barrier = pltpu.get_barrier_semaphore()

    def greet(p, carry):
        peer = lax.rem(me + p, n)
        pl.semaphore_signal(barrier, inc=1, device_id=device(peer), device_id_type=MESH)
        return carry

    lax.fori_loop(1, n, greet, 0)
    pl.semaphore_wait(barrier, n - 1)
    own = o_ref.at[pl.ds(me * rows, rows)]
    pltpu.make_async_copy(x_ref, own, recv_sem).start()

    def send(p, carry):
        peer = lax.rem(me + p, n)
        pltpu.make_async_remote_copy(
            src_ref=x_ref,
            dst_ref=own,
            send_sem=send_sem,
            recv_sem=recv_sem,
            device_id=device(peer),
            device_id_type=MESH,
        ).start()
        return carry

    lax.fori_loop(1, n, send, 0)
    sent = o_ref.at[pl.ds(0, (n - 1) * rows)]
    pltpu.make_async_copy(sent, sent, send_sem).wait()
    pltpu.make_async_copy(o_ref, o_ref, recv_sem).wait()


def gather_rows(x, axis, collective_id):
    n = lax.axis_size(axis)
    rows, cols = x.shape
    return pl.pallas_call(
        functools.partial(_gather_kernel, axis),
        out_shape=jax.ShapeDtypeStruct((n * rows, cols), x.dtype),
        in_specs=[pl.BlockSpec(memory_space=pl.ANY)],
        out_specs=pl.BlockSpec(memory_space=pl.ANY),
        scratch_shapes=[pltpu.SemaphoreType.DMA(()), pltpu.SemaphoreType.DMA(())],
        compiler_params=pltpu.CompilerParams(collective_id=collective_id, has_side_effects=True),
    )(x)


def _exchange_kernel(axis, x_ref, o_ref, send_sem, recv_sem):
    coords = {name: lax.axis_index(name) for name in ("g", "c", "mp")}
    if axis == "dp":
        cores = lax.axis_size("c")
        n = lax.axis_size("g") * cores
        me = coords["g"] * cores + coords["c"]

        def device(peer):
            return (peer // cores, peer % cores, coords["mp"])

    else:
        n = lax.axis_size(axis)
        me = coords[axis]

        def device(peer):
            return tuple(peer if name == axis else coords[name] for name in ("g", "c", "mp"))

    barrier = pltpu.get_barrier_semaphore()

    def greet(p, carry):
        peer = lax.rem(me + p, n)
        pl.semaphore_signal(barrier, inc=1, device_id=device(peer), device_id_type=MESH)
        return carry

    lax.fori_loop(1, n, greet, 0)
    pl.semaphore_wait(barrier, n - 1)
    pltpu.make_async_copy(x_ref.at[me], o_ref.at[me], recv_sem).start()

    def send(p, carry):
        peer = lax.rem(me + p, n)
        pltpu.make_async_remote_copy(
            src_ref=x_ref.at[peer],
            dst_ref=o_ref.at[me],
            send_sem=send_sem,
            recv_sem=recv_sem,
            device_id=device(peer),
            device_id_type=MESH,
        ).start()
        return carry

    lax.fori_loop(1, n, send, 0)
    sent = o_ref.at[pl.ds(0, n - 1)]
    pltpu.make_async_copy(sent, sent, send_sem).wait()
    pltpu.make_async_copy(o_ref, o_ref, recv_sem).wait()


def exchange(x, axis, collective_id):
    return pl.pallas_call(
        functools.partial(_exchange_kernel, axis),
        out_shape=jax.ShapeDtypeStruct(x.shape, x.dtype),
        in_specs=[pl.BlockSpec(memory_space=pl.ANY)],
        out_specs=pl.BlockSpec(memory_space=pl.ANY),
        scratch_shapes=[pltpu.SemaphoreType.DMA(()), pltpu.SemaphoreType.DMA(())],
        compiler_params=pltpu.CompilerParams(collective_id=collective_id, has_side_effects=True),
    )(x)


def reduce_scatter_mp(blocks, collective_id):
    return jnp.sum(exchange(blocks, "mp", collective_id), axis=0)


def swap_halves(value, tok_rows):
    return lax.all_to_all(
        value.reshape(2, tok_rows, value.shape[1]), "c", split_axis=0, concat_axis=0, tiled=True
    )


def natural_blocks(halves, mp_count):
    _, rows, cols = halves.shape
    pairs = lax.axis_size("g")
    width = cols // pairs
    ordered = jnp.transpose(halves.reshape(2, rows, pairs, width), (1, 2, 0, 3))
    return jnp.transpose(ordered.reshape(rows, mp_count, -1), (1, 0, 2))


def local(
    attention,
    residual,
    out_weight,
    ffn_gain,
    shared_gate,
    shared_up,
    shared_down,
    expert_gate,
    expert_up,
    expert_down,
    route_ids,
    route_scores,
    placement,
    next_gain,
):
    dp = ("g", "c")
    tok_rows = attention.shape[0]
    top_count = route_ids.shape[1]
    mp_count = lax.axis_size("mp")
    pairs = lax.axis_size("g")
    experts = pairs * lax.axis_size("c")
    core = lax.axis_index("c")
    capacity = min(tok_rows, 8 * tok_rows // experts)
    model_width = D
    block_width = model_width // mp_count

    w_half = gather_rows(out_weight.T, "g", 0)
    att_pair = lax.all_gather(attention, "c", axis=0, tiled=True)
    part_half = matmul_t(att_pair, w_half)
    partial_value = natural_blocks(swap_halves(part_half, tok_rows), mp_count)
    gain_row = jnp.broadcast_to(ffn_gain[None, None, :], (mp_count, 1, block_width))
    exchanged = exchange(jnp.concatenate([partial_value, gain_row], axis=1), "mp", 3)
    projected = jnp.sum(exchanged[:, :tok_rows, :], axis=0)
    gain = exchanged[:, tok_rows, :].reshape(model_width)
    hidden = (residual.astype(jnp.float32) + projected).astype(jnp.bfloat16)
    hidden_float = hidden.astype(jnp.float32)
    hidden_blocks = gather_rows(hidden, "mp", 1).reshape(mp_count, tok_rows, block_width)
    whole_hidden = jnp.transpose(hidden_blocks, (1, 0, 2)).reshape(tok_rows, model_width)
    whole_hidden = whole_hidden.astype(jnp.float32)
    squares = jnp.sum(whole_hidden * whole_hidden, axis=1)
    scale = lax.rsqrt(squares / model_width + EPSILON)[:, None]
    whole_rows = (whole_hidden * scale * gain).astype(jnp.bfloat16)
    normed = (hidden_float * scale * ffn_gain).astype(jnp.bfloat16)

    flat_ids = route_ids.reshape(-1)
    expert_iota = jnp.arange(experts, dtype=jnp.int32)
    one_hot = (flat_ids[:, None] == expert_iota[None, :]).astype(jnp.int32)
    target = jnp.sum(one_hot * placement[None, :], axis=1)
    slot = jnp.sum((jnp.cumsum(one_hot, axis=0) - one_hot) * one_hot, axis=1)
    dest = target * capacity + slot
    slots = experts * capacity
    hit = (dest[:, None] == jnp.arange(slots, dtype=jnp.int32)[None, :]).reshape(
        tok_rows, top_count, slots
    )
    flat_scores = route_scores.reshape(tok_rows, top_count)
    combine = jnp.sum(jnp.where(hit, flat_scores[:, :, None], 0.0), axis=1)
    pick = jnp.any(hit, axis=1).astype(jnp.bfloat16)
    half = block_width // 2
    gate_block = expert_gate[0].reshape(mp_count, block_width, -1)
    up_block = expert_up[0].reshape(mp_count, block_width, -1)
    gate_val = None
    up_val = None
    for part in range(2):
        columns = slice(part * half, (part + 1) * half)
        outgoing = matmul(pick.T, normed[:, columns]).astype(jnp.bfloat16)
        arrived = exchange(outgoing.reshape(experts, capacity, half), "dp", 5 + part)
        copies = jnp.broadcast_to(arrived.reshape(1, slots, half), (mp_count, slots, half))
        in_rows = lax.all_to_all(copies, "mp", split_axis=0, concat_axis=0, tiled=True)
        gate_part = jnp.einsum(
            "qsf,qfh->sh", in_rows, gate_block[:, columns, :], preferred_element_type=jnp.float32
        )
        up_part = jnp.einsum(
            "qsf,qfh->sh", in_rows, up_block[:, columns, :], preferred_element_type=jnp.float32
        )
        gate_val = gate_part if gate_val is None else gate_val + gate_part
        up_val = up_part if up_val is None else up_val + up_part
    activated = (jax.nn.silu(gate_val) * up_val).astype(jnp.bfloat16)
    down_block = expert_down[0].reshape(-1, mp_count, block_width)
    partial_out = jnp.einsum(
        "sh,hqf->qsf", activated, down_block, preferred_element_type=jnp.float32
    ).astype(jnp.bfloat16)
    summed = lax.all_to_all(partial_out, "mp", split_axis=0, concat_axis=0, tiled=True)
    expert_out = jnp.sum(summed.astype(jnp.float32), axis=0).astype(jnp.bfloat16)
    returned = lax.all_to_all(
        expert_out.reshape(experts, capacity, block_width),
        dp,
        split_axis=0,
        concat_axis=0,
        tiled=True,
    ).reshape(slots, block_width)
    routed = jnp.dot(
        combine,
        returned.astype(jnp.float32),
        precision=lax.Precision.HIGHEST,
        preferred_element_type=jnp.float32,
    )

    hidden_units = shared_gate.shape[1]
    shared_shard, _ = lax.optimization_barrier(
        (jnp.concatenate([shared_gate, shared_up, shared_down.T], axis=1), arrived)
    )
    shared_all = lax.all_gather(shared_shard, dp, axis=0, tiled=True)
    shared_gval = matmul(whole_rows, shared_all[:, :hidden_units])
    shared_uval = matmul(whole_rows, shared_all[:, hidden_units : 2 * hidden_units])
    shared_act = (jax.nn.silu(shared_gval) * shared_uval).astype(jnp.bfloat16)
    shared_part = jnp.einsum(
        "th,qfh->qtf",
        shared_act,
        shared_all[:, 2 * hidden_units :].reshape(mp_count, block_width, hidden_units),
        preferred_element_type=jnp.float32,
    )
    mixture = reduce_scatter_mp(shared_part, 4) + routed
    final = (hidden_float + mixture).astype(jnp.bfloat16)
    final_float = final.astype(jnp.float32)
    own_squares = jnp.sum(final_float * final_float, axis=1)
    square_rows = jnp.broadcast_to(own_squares[None, :], (8, tok_rows))
    final_squares = jnp.sum(
        gather_rows(square_rows, "mp", 2).reshape(mp_count, 8, tok_rows)[:, 0, :], axis=0
    )
    next_normed = (
        final_float * lax.rsqrt(final_squares / model_width + EPSILON)[:, None] * next_gain
    ).astype(jnp.bfloat16)
    return (final, next_normed)


def solution(mesh):
    dp_count, mp_count = mesh.devices.shape
    paired = Mesh(mesh.devices.reshape(dp_count // 2, 2, mp_count), ("g", "c", "mp"))
    dp = ("g", "c")
    in_specs = (
        P(dp, "mp"),
        P(dp, "mp"),
        P("mp", dp),
        P("mp"),
        P(dp, "mp"),
        P(dp, "mp"),
        P("mp", dp),
        P(dp, None, "mp"),
        P(dp, None, "mp"),
        P(dp, "mp", None),
        P(dp, None),
        P(dp, None),
        P(),
        P("mp"),
    )
    out_specs = (P(dp, "mp"), P(dp, "mp"))
    return jax.shard_map(local, mesh=paired, in_specs=in_specs, out_specs=out_specs, check_vma=False)
```
